32 devices in a mesh: shard: 8 (over z, x), replica: 4 (over y, core).
Axes of the slice: x: 2, y: 2, z: 4, core: 2. Of those that a mesh axis runs over, the one named last changes fastest.
Arguments:
- momentum: bfloat16 [1, 4, 4096, 4096], P(None, 'replica', 'shard'), may hold values from -36 to 36
- grad: bfloat16 [1, 4, 4096, 4096], P(None, 'replica', 'shard'), may hold values from -6 to 6
- right_prev: bfloat16 [1, 4096, 256], P(None, 'shard'), may hold values from -6 to 6
Outputs:
- momentum_new: bfloat16 [1, 4, 4096, 4096], P(None, 'replica', 'shard')
- update: bfloat16 [1, 4096, 4096], P(None, 'shard')
- right_factor: bfloat16 [1, 4096, 256], P(None, 'shard')
The draws below stay inside these ranges and needn't reach their ends.
All inputs are finite; a program needn't handle non-finite values.
Results may differ from the reference program's by a relative error of at most 0.0095.
Values may be sent and summed in bfloat16 or wider, within the bound.
A program may use at most 64 MiB of HBM per device.

```python
import math
import jax
import jax.numpy as jnp
from jax import lax

D = 4096
RANK = 256
LAYERS = 1
REPLICAS = 4
N_REPLICA = 4


def draw_momentum(key, part):
    key_base = jax.random.fold_in(key, 11)
    key_rows = jax.random.fold_in(key, 12)
    key_cols = jax.random.fold_in(key, 13)
    position = jnp.arange(D, dtype=jnp.float32) / D
    rising = jnp.exp(jnp.log(3.0) * position)
    base = jnp.clip(jax.random.normal(key_base, (LAYERS, REPLICAS, D, D), jnp.float32), -6.0, 6.0)
    row_rough = jnp.exp(jax.random.uniform(key_rows, (LAYERS, REPLICAS, D, 1), jnp.float32, jnp.log(0.7), jnp.log(1.4)))
    col_rough = jnp.exp(jax.random.uniform(key_cols, (LAYERS, REPLICAS, 1, D), jnp.float32, jnp.log(0.7), jnp.log(1.4)))
    row_scale = rising[:, None] * row_rough
    col_scale = rising[None, :] * col_rough
    values = jnp.clip(base * row_scale * col_scale, -36.0, 36.0)
    return values.astype(jnp.bfloat16)


def with_spikes(entries, key, source, target, blocks, factor):
    def block_of(axis_at):
        return (jnp.arange(entries.shape[axis_at]) // (entries.shape[axis_at] // blocks)).reshape((-1,) + (1,) * (entries.ndim - 1 - axis_at))

    near = jax.random.permutation(key, blocks)[block_of(target)]
    far = (block_of(target) + blocks // 2) % blocks
    return jnp.where((block_of(source) == near) | (block_of(source) == far), factor * entries, entries)


def block_levels(own_key, dims, pieces, smallest, high):
    def one(dim, parts):
        steps = jax.random.uniform(jax.random.fold_in(jax.random.fold_in(own_key, 6), dim), (parts,), jnp.float32, smallest / len(pieces), high / len(pieces))
        return jnp.repeat(jnp.exp(steps), dims[dim] // parts).reshape((-1,) + (1,) * (len(dims) - dim - 1))

    loudness = one(*pieces[0])
    for cut in pieces[1:]:
        loudness = loudness * one(*cut)
    return loudness


def centred(rng, shape, scale, reach, pieces=(), held_as=jnp.bfloat16):
    drawn = scale * jax.random.normal(rng, shape, jnp.float32)
    if pieces:
        drawn = drawn * block_levels(rng, shape, pieces, -0.22, 0.18)
    return jnp.clip(drawn, -reach, reach).astype(held_as)


def heavy_noise(stream_key, dims, scale, bound, pieces, heavy, kind=jnp.bfloat16):
    entries = scale * jax.random.normal(stream_key, dims, jnp.float32)
    if pieces:
        entries = entries * block_levels(stream_key, dims, pieces, -0.22, 0.18)
    return jnp.clip(with_spikes(entries, jax.random.fold_in(stream_key, 3), *heavy), -bound, bound).astype(kind)


def setup_inputs(seed: int = 0) -> dict:
    streams_of = jax.random.split(jax.random.key(seed), 4)
    momentum = draw_momentum(jax.random.fold_in(streams_of[3], 71), 0)
    grad = heavy_noise(streams_of[1], (LAYERS, REPLICAS, D, D), 1.0, 6.0, ((1, 4), (2, 8)), (2, 3, 8, 2.0))
    right_prev = centred(streams_of[2], (LAYERS, D, RANK), 1.0, 6.0, ((1, 8),))
    return {"momentum": momentum, "grad": grad, "right_prev": right_prev}


momentum_decay = 0.95
epsilon_norm = 1e-06

def reference(momentum, grad, right_prev):
    momenta = []
    updates = []
    rights = []
    for layer in range(LAYERS):
        buffers = []
        for member in range(N_REPLICA):
            buffers.append(momentum[layer, member].astype(jnp.float32) + grad[layer, member].astype(jnp.float32))
        buffers_b = [value.astype(jnp.bfloat16) for value in buffers]
        left = jnp.zeros((D, RANK), jnp.float32)
        for member in range(N_REPLICA):
            left = left + jnp.dot(buffers_b[member].astype(jnp.float32), right_prev[layer].astype(jnp.float32), preferred_element_type=jnp.float32)
        gram = jnp.dot(left.T, left, precision=lax.Precision.HIGHEST)
        chol = jnp.linalg.cholesky(gram)
        ortho = lax.linalg.triangular_solve(chol, left, left_side=False, lower=True, transpose_a=True)
        ortho_b = ortho.astype(jnp.bfloat16)
        right = jnp.zeros((D, RANK), jnp.float32)
        for member in range(N_REPLICA):
            right = right + jnp.dot(buffers_b[member].T.astype(jnp.float32), ortho_b.astype(jnp.float32), preferred_element_type=jnp.float32)
        right = right / N_REPLICA
        right_b = right.astype(jnp.bfloat16)
        norms = jnp.sqrt(lax.optimization_barrier(jnp.sum(right * right, axis=0)) + epsilon_norm)
        factor = D / math.sqrt(RANK)
        scaled = (ortho * (factor / norms)).astype(jnp.bfloat16)
        feedback = jnp.dot(ortho_b.astype(jnp.float32), right_b.T.astype(jnp.float32), preferred_element_type=jnp.float32)
        layer_momenta = []
        for member in range(N_REPLICA):
            layer_momenta.append((buffers[member] - (1.0 - momentum_decay) * feedback).astype(jnp.bfloat16))
        momenta.append(jnp.stack(layer_momenta))
        updates.append(jnp.dot(scaled.astype(jnp.float32), right_b.T.astype(jnp.float32), preferred_element_type=jnp.float32).astype(jnp.bfloat16))
        rights.append(right_b)
    return (jnp.stack(momenta), jnp.stack(updates), jnp.stack(rights))
```

```python
import functools
import math

import jax
import jax.numpy as jnp
from jax import lax
from jax.experimental import pallas as pl
from jax.experimental.pallas import tpu as pltpu
from jax.sharding import PartitionSpec as P

momentum_decay = 0.95
epsilon_norm = 1e-06
MESH = pl.DeviceIdType.MESH
HIGHEST = lax.Precision.HIGHEST
F32 = jnp.float32
BF16 = jnp.bfloat16
BLOCK = 32
MAX_COPIES = 96


def grid_of(shards_n, replicas_n):
    x = math.isqrt(shards_n // 2)
    if x < 1 or 2 * x * x != shards_n:
        x = 1
    c = 2 if replicas_n % 2 == 0 else 1
    return shards_n // x, x, replicas_n // c, c


class Net:
    def __init__(self, dims, send, recv):
        self.dims = dims
        _, nx, _, nc = dims
        s = lax.axis_index("shard")
        r = lax.axis_index("replica")
        self.at = [s // nx, s % nx, r // nc, r % nc]
        self.send, self.recv, self.used = send, recv, 0

    def device(self, axis, coordinate):
        place = list(self.at)
        place[axis] = coordinate
        return {
            "shard": place[0] * self.dims[1] + place[1],
            "replica": place[2] * self.dims[3] + place[3],
        }

    def peers(self, axis):
        n, me = self.dims[axis], self.at[axis]
        return [((me + d) % n, (me + n - d) % n) for d in range(1, n)]

    def barrier(self):
        sem = pltpu.get_barrier_semaphore()
        count = 0
        for axis in range(4):
            for target, _ in self.peers(axis):
                pl.semaphore_signal(sem, inc=1, device_id=self.device(axis, target), device_id_type=MESH)
                count += 1
        pl.semaphore_wait(sem, count)

    def start(self, src, dst, axis, target):
        i = self.used
        self.used += 1
        copy = pltpu.make_async_remote_copy(
            src_ref=src,
            dst_ref=dst,
            send_sem=self.send.at[i],
            recv_sem=self.recv.at[i],
            device_id=self.device(axis, target),
            device_id_type=MESH,
        )
        copy.start()
        return copy


def gather_all(net, own, out):
    z, x, y, c = net.at
    half = out.shape[-1] // 2
    a, b = pl.ds(0, half), pl.ds(half, half)
    others = net.peers(3)
    sent = []

    def forward(view):
        for oc, _ in others:
            sent.append(net.start(view, view, 3, oc))

    first = [(net.start(own, out.at[z, x, y, c], 0, t), f) for t, f in net.peers(0)]
    for oc, _ in others:
        sent.append(net.start(own, out.at[z, x, y, c], 3, oc))
    for copy, f in first:
        copy.wait()
    for copy, f in first:
        forward(out.at[f, x, y, c])
    mine_a, mine_b = out.at[:, x, y, c, :, a], out.at[:, x, y, c, :, b]
    second = [(net.start(mine_a, mine_a, 1, t), out.at[:, f, y, c, :, a]) for t, f in net.peers(1)]
    second += [(net.start(mine_b, mine_b, 2, t), out.at[:, x, f, c, :, b]) for t, f in net.peers(2)]
    for copy, _ in second:
        copy.wait()
    mine_a, mine_b = out.at[:, :, y, c, :, a], out.at[:, x, :, c, :, b]
    third = [(net.start(mine_a, mine_a, 2, t), out.at[:, :, f, c, :, a]) for t, f in net.peers(2)]
    third += [(net.start(mine_b, mine_b, 1, t), out.at[:, f, :, c, :, b]) for t, f in net.peers(1)]
    for _, view in second:
        forward(view)
    for copy, _ in third:
        copy.wait()
    for _, view in third:
        forward(view)
    for copy in sent:
        copy.wait()


def gather_kernel(dims, block, out, send, recv, local):
    net = Net(dims, send, recv)
    z, x, y, c = net.at
    own = pltpu.make_async_copy(block.at[y, c], out.at[z, x, y, c], local)
    own.start()
    net.barrier()
    own.wait()
    gather_all(net, block.at[y, c], out)


def left_kernel(dims, part, left, gram, rc, acc, ry, g, rgc, g1, rgy, g2, rgx, g3, gz, send, recv):
    net = Net(dims, send, recv)
    z, x, y, c = net.at
    net.barrier()
    copies = [net.start(part.at[:, t], rc.at[d], 3, t) for d, (t, _) in enumerate(net.peers(3))]
    for copy in copies:
        copy.wait()
    total = part[:, c]
    for d in range(len(copies)):
        total = total + rc[d]
    acc[...] = total
    copies = [net.start(acc.at[t], ry.at[d], 2, t) for d, (t, _) in enumerate(net.peers(2))]
    for copy in copies:
        copy.wait()
    own = acc[y]
    for d in range(len(copies)):
        own = own + ry[d]
    left[y, c] = own
    rows = [net.start(left.at[y, c], left.at[y, c], 2, t) for t, _ in net.peers(2)]
    product = lax.dot_general(own, own, (((0,), (0,)), ((), ())), precision=HIGHEST, preferred_element_type=F32)
    g[...] = product.reshape(g.shape)
    copies = [net.start(g.at[t], rgc.at[d], 3, t) for d, (t, _) in enumerate(net.peers(3))]
    for copy in copies:
        copy.wait()
    total = g[c]
    for d in range(len(copies)):
        total = total + rgc[d]
    g1[...] = total
    copies = [net.start(g1.at[t], rgy.at[d], 2, t) for d, (t, _) in enumerate(net.peers(2))]
    for copy in copies:
        copy.wait()
    total = g1[y]
    for d in range(len(copies)):
        total = total + rgy[d]
    g2[...] = total
    copies = [net.start(g2.at[t], rgx.at[d], 1, t) for d, (t, _) in enumerate(net.peers(1))]
    for copy in rows:
        copy.wait()
    rows = [net.start(left.at[:, c], left.at[:, c], 3, t) for t, _ in net.peers(3)]
    for copy in copies:
        copy.wait()
    total = g2[x]
    for d in range(len(copies)):
        total = total + rgx[d]
    g3[...] = total
    gz[z] = total
    copies = [net.start(g3, gz.at[z], 0, t) for t, _ in net.peers(0)]
    for copy in copies:
        copy.wait()
    total = gz[0]
    for d in range(1, dims[0]):
        total = total + gz[d]
    gram[c, y, x] = total
    for axis, view in ((1, gram.at[c, y, x]), (2, gram.at[c, y]), (3, gram.at[c])):
        copies = [net.start(view, view, axis, t) for t, _ in net.peers(axis)]
        for copy in copies:
            copy.wait()
    for copy in rows:
        copy.wait()


def ortho_kernel(gram, left, ortho, work, inverse):
    n = gram.shape[0]
    row = lax.broadcasted_iota(jnp.int32, (n, n), 0)
    col = lax.broadcasted_iota(jnp.int32, (n, n), 1)
    work[:, :n] = gram[...]
    work[:, n:] = jnp.where(row == col, 1.0, 0.0).astype(F32)
    ids = lax.broadcasted_iota(jnp.int32, (BLOCK, 2 * BLOCK), 0)
    lanes = lax.broadcasted_iota(jnp.int32, (BLOCK, BLOCK), 1)
    eye = jnp.where(lax.broadcasted_iota(jnp.int32, (BLOCK, BLOCK), 0) == lanes, 1.0, 0.0).astype(F32)
    for k in range(n // BLOCK):
        lo, hi = k * BLOCK, (k + 1) * BLOCK
        v = jnp.concatenate([work[lo:hi, lo:hi], eye], axis=1)
        for j in range(BLOCK):
            scale = lax.rsqrt(v[j : j + 1, j : j + 1])
            pivot = v[j : j + 1, :] * scale
            column = v[:, j : j + 1] * scale
            v = jnp.where(ids == j, pivot, v - jnp.where(ids > j, column * pivot, 0.0))
        upper = jnp.dot(v[:, BLOCK:], work[lo:hi, :], precision=HIGHEST, preferred_element_type=F32)
        inverse[lo:hi, :] = upper[:, n:]
        if hi < n:
            work[hi:, :] -= lax.dot_general(
                upper[:, hi:n], upper, (((0,), (0,)), ((), ())), precision=HIGHEST, preferred_element_type=F32
            )
    ortho[...] = lax.dot_general(
        left[...], inverse[...], (((1,), (1,)), ((), ())), precision=HIGHEST, preferred_element_type=F32
    )


def right_kernel(dims, part, out, sc, rc, acc, sya, rya, sxb, rxb, a2, b2, sxa, rxa, syb, ryb, a3, sz, rz, own, send, recv):
    net = Net(dims, send, recv)
    nz, nx, ny, nc = dims
    z, x, y, c = net.at
    half = part.shape[-1] // 2
    a, b = slice(0, half), slice(half, 2 * half)
    net.barrier()
    copies = []
    for i in range(nz):
        for d, (t, _) in enumerate(net.peers(3)):
            sc[d, i] = part[i, :, :, t].astype(BF16)
            copies.append(net.start(sc.at[d, i], rc.at[d, i], 3, t))
    for copy in copies:
        copy.wait()
    for i in range(nz):
        total = part[i, :, :, c]
        for d in range(nc - 1):
            total = total + rc[d, i].astype(F32)
        acc[i] = total
    copies = []
    for d, (t, _) in enumerate(net.peers(2)):
        sya[d] = acc[:, :, t, :, a].astype(BF16)
        copies.append(net.start(sya.at[d], rya.at[d], 2, t))
    for d, (t, _) in enumerate(net.peers(1)):
        sxb[d] = acc[:, t, :, :, b].astype(BF16)
        copies.append(net.start(sxb.at[d], rxb.at[d], 1, t))
    for copy in copies:
        copy.wait()
    total = acc[:, :, y, :, a]
    for d in range(ny - 1):
        total = total + rya[d].astype(F32)
    a2[...] = total
    total = acc[:, x, :, :, b]
    for d in range(nx - 1):
        total = total + rxb[d].astype(F32)
    b2[...] = total
    copies = []
    for d, (t, _) in enumerate(net.peers(1)):
        sxa[d] = a2[:, t].astype(BF16)
        copies.append(net.start(sxa.at[d], rxa.at[d], 1, t))
    for d, (t, _) in enumerate(net.peers(2)):
        syb[d] = b2[:, t].astype(BF16)
        copies.append(net.start(syb.at[d], ryb.at[d], 2, t))
    for copy in copies:
        copy.wait()
    total = a2[:, x]
    for d in range(nx - 1):
        total = total + rxa[d].astype(F32)
    a3[:, :, a] = total
    total = b2[:, y]
    for d in range(ny - 1):
        total = total + ryb[d].astype(F32)
    a3[:, :, b] = total
    copies = []
    for d, (t, _) in enumerate(net.peers(0)):
        sz[d] = a3[t].astype(BF16)
        copies.append(net.start(sz.at[d], rz.at[d], 0, t))
    for copy in copies:
        copy.wait()
    total = a3[z]
    for d in range(nz - 1):
        total = total + rz[d].astype(F32)
    mine = (total * (1.0 / (ny * nc))).astype(BF16)
    own[...] = mine
    out[z, x, y, c] = mine
    gather_all(net, own, out)


def call(kernel, dims, identity, operands, outs, scratch, local=False):
    vmem = pl.BlockSpec(memory_space=pltpu.VMEM)
    sems = [pltpu.SemaphoreType.DMA((MAX_COPIES,))] * 2
    if local:
        sems = sems + [pltpu.SemaphoreType.DMA]
    single = not isinstance(outs, tuple)
    return pl.pallas_call(
        functools.partial(kernel, dims),
        out_shape=outs,
        in_specs=[vmem] * len(operands),
        out_specs=vmem if single else (vmem,) * len(outs),
        scratch_shapes=[pltpu.VMEM(shape, kind) for shape, kind in scratch] + sems,
        compiler_params=pltpu.CompilerParams(
            collective_id=identity, has_side_effects=True, vmem_limit_bytes=48 << 20
        ),
    )(*operands)


def gather(dims, block, rows, rank):
    nz, nx, ny, nc = dims
    piece = rows // (ny * nc)
    full = call(
        gather_kernel, dims, 0, (block.reshape(ny, nc, piece, rank),),
        jax.ShapeDtypeStruct((nz, nx, ny, nc, piece, rank), BF16), [], local=True,
    )
    return full.reshape(rows * nz * nx, rank)


def sum_left(dims, part):
    nz, nx, ny, nc = dims
    rows, rank = part.shape
    piece = rows // (ny * nc)
    g = rank // (nc * ny * nx)
    pc, py, px = max(nc - 1, 1), max(ny - 1, 1), max(nx - 1, 1)
    left, gram = call(
        left_kernel, dims, 1, (part.reshape(ny, nc, piece, rank),),
        (jax.ShapeDtypeStruct((ny, nc, piece, rank), F32), jax.ShapeDtypeStruct((nc, ny, nx, g, rank), F32)),
        [
            ((pc, ny, piece, rank), F32), ((ny, piece, rank), F32), ((py, piece, rank), F32),
            ((nc, ny, nx, g, rank), F32), ((pc, ny, nx, g, rank), F32), ((ny, nx, g, rank), F32),
            ((py, nx, g, rank), F32), ((nx, g, rank), F32), ((px, g, rank), F32), ((g, rank), F32),
            ((nz, g, rank), F32),
        ],
    )
    return left.reshape(rows, rank), gram.reshape(rank, rank)


def sum_right(dims, part):
    nz, nx, ny, nc = dims
    width, rank = part.shape
    piece = width // (nz * nx * ny * nc)
    half = rank // 2
    pc, py, px, pz = max(nc - 1, 1), max(ny - 1, 1), max(nx - 1, 1), max(nz - 1, 1)
    two = lambda shape, kind: [(shape, kind), (shape, kind)]
    full = call(
        right_kernel, dims, 2, (part.reshape(nz, nx, ny, nc, piece, rank),),
        jax.ShapeDtypeStruct((nz, nx, ny, nc, piece, rank), BF16),
        two((pc, nz, nx, ny, piece, rank), BF16)
        + [((nz, nx, ny, piece, rank), F32)]
        + two((py, nz, nx, piece, half), BF16)
        + two((px, nz, ny, piece, half), BF16)
        + [((nz, nx, piece, half), F32), ((nz, ny, piece, half), F32)]
        + two((px, nz, piece, half), BF16)
        + two((py, nz, piece, half), BF16)
        + [((nz, piece, rank), F32)]
        + two((pz, piece, rank), BF16)
        + [((piece, rank), BF16)],
    )
    return full.reshape(width, rank)


def orthonormal(gram, left):
    rank = gram.shape[0]
    vmem = pl.BlockSpec(memory_space=pltpu.VMEM)
    return pl.pallas_call(
        ortho_kernel,
        out_shape=jax.ShapeDtypeStruct(left.shape, F32),
        in_specs=[vmem, vmem],
        out_specs=vmem,
        scratch_shapes=[pltpu.VMEM((rank, 2 * rank), F32), pltpu.VMEM((rank, rank), F32)],
        compiler_params=pltpu.CompilerParams(vmem_limit_bytes=32 << 20),
    )(gram, left)


def shards(dims, momentum, grad, right_prev):
    rows = grad.shape[2]
    width = grad.shape[3]
    rank = right_prev.shape[2]
    factor = width / math.sqrt(rank)
    buffer = momentum[0, 0].astype(F32) + grad[0, 0].astype(F32)
    buffer_b = buffer.astype(BF16)
    local_left = jnp.dot(buffer_b, gather(dims, right_prev[0], rows, rank), preferred_element_type=F32)
    summed, gram = sum_left(dims, local_left)
    ortho = orthonormal(gram, summed)
    ortho_b = ortho.astype(BF16)
    part = lax.dot_general(buffer_b, ortho_b, (((0,), (0,)), ((), ())), preferred_element_type=F32)
    right_full = sum_right(dims, part)
    wide = right_full.astype(F32)
    norms = jnp.sqrt(jnp.sum(wide * wide, axis=0) + epsilon_norm)
    right_own = lax.dynamic_slice_in_dim(right_full, lax.axis_index("shard") * rows, rows, axis=0)
    scaled = (ortho * (factor / norms)).astype(BF16)
    feedback = lax.dot_general(ortho_b, right_full, (((1,), (1,)), ((), ())), preferred_element_type=F32)
    momentum_new = (buffer - (1.0 - momentum_decay) * feedback).astype(BF16)
    stepped = lax.dot_general(scaled, right_full, (((1,), (1,)), ((), ())), preferred_element_type=F32)
    return momentum_new[None, None], stepped.astype(BF16)[None], right_own[None]


def solution(mesh):
    dims = grid_of(mesh.shape["shard"], mesh.shape["replica"])
    return jax.shard_map(
        functools.partial(shards, dims),
        mesh=mesh,
        in_specs=(
            P(None, "replica", "shard", None),
            P(None, "replica", "shard", None),
            P(None, "shard", None),
        ),
        out_specs=(
            P(None, "replica", "shard", None),
            P(None, "shard", None),
            P(None, "shard", None),
        ),
        check_vma=False,
    )
```

```python
import functools
import math

import jax
import jax.numpy as jnp
from jax import lax
from jax.experimental import pallas as pl
from jax.experimental.pallas import tpu as pltpu
from jax.sharding import PartitionSpec as P

momentum_decay = 0.95
epsilon_norm = 1e-06
MESH = pl.DeviceIdType.MESH
HIGHEST = lax.Precision.HIGHEST
F32 = jnp.float32
BF16 = jnp.bfloat16
BLOCK = 64
PIVOTS = 4
CHUNKS = 8
MAX_COPIES = 96


def grid_of(shards_n, replicas_n):
    x = math.isqrt(shards_n // 2)
    if x < 1 or 2 * x * x != shards_n:
        x = 1
    c = 2 if replicas_n % 2 == 0 else 1
    return shards_n // x, x, replicas_n // c, c


class Net:
    def __init__(self, dims, send, recv):
        self.dims = dims
        _, nx, _, nc = dims
        s = lax.axis_index("shard")
        r = lax.axis_index("replica")
        self.at = [s // nx, s % nx, r // nc, r % nc]
        self.send, self.recv, self.used = send, recv, 0

    def device(self, axis, coordinate):
        place = list(self.at)
        place[axis] = coordinate
        return {
            "shard": place[0] * self.dims[1] + place[1],
            "replica": place[2] * self.dims[3] + place[3],
        }

    def peers(self, axis):
        n, me = self.dims[axis], self.at[axis]
        return [((me + d) % n, (me + n - d) % n) for d in range(1, n)]

    def barrier(self):
        sem = pltpu.get_barrier_semaphore()
        count = 0
        for axis in range(4):
            for target, _ in self.peers(axis):
                pl.semaphore_signal(sem, inc=1, device_id=self.device(axis, target), device_id_type=MESH)
                count += 1
        pl.semaphore_wait(sem, count)

    def start(self, src, dst, axis, target):
        i = self.used
        self.used += 1
        copy = pltpu.make_async_remote_copy(
            src_ref=src,
            dst_ref=dst,
            send_sem=self.send.at[i],
            recv_sem=self.recv.at[i],
            device_id=self.device(axis, target),
            device_id_type=MESH,
        )
        copy.start()
        return copy


def gather_all(net, own, out, work=None):
    z, x, y, c = net.at
    half = out.shape[0] // 2
    a, b = pl.ds(0, half), pl.ds(half, out.shape[0] - half)
    others = net.peers(3)
    sent = []

    def forward(view):
        for oc, _ in others:
            sent.append(net.start(view, view, 3, oc))

    first = [(net.start(own, out.at[z, x, y, c], 0, t), f) for t, f in net.peers(0)]
    for oc, _ in others:
        sent.append(net.start(own, out.at[z, x, y, c], 3, oc))
    if work is not None:
        work()
    for copy, f in first:
        copy.wait()
    for copy, f in first:
        forward(out.at[f, x, y, c])
    mine_a, mine_b = out.at[a, x, y, c], out.at[b, x, y, c]
    second = [(net.start(mine_a, mine_a, 1, t), out.at[a, f, y, c]) for t, f in net.peers(1)]
    second += [(net.start(mine_b, mine_b, 2, t), out.at[b, x, f, c]) for t, f in net.peers(2)]
    for copy, _ in second:
        copy.wait()
    mine_a, mine_b = out.at[a, :, y, c], out.at[b, x, :, c]
    third = [(net.start(mine_a, mine_a, 2, t), out.at[a, :, f, c]) for t, f in net.peers(2)]
    third += [(net.start(mine_b, mine_b, 1, t), out.at[b, f, :, c]) for t, f in net.peers(1)]
    for _, view in second:
        forward(view)
    for copy, _ in third:
        copy.wait()
    for _, view in third:
        forward(view)
    for copy in sent:
        copy.wait()


def gather_kernel(dims, block, momentum, grad, out, buffer, m, g, send, recv, local):
    net = Net(dims, send, recv)
    z, x, y, c = net.at
    own = pltpu.make_async_copy(block.at[y, c], out.at[z, x, y, c], local.at[0])
    own.start()
    loads = []
    for k in range(CHUNKS):
        size = buffer.shape[0] // CHUNKS
        rows = pl.ds(k * size, size)
        pair = [
            pltpu.make_async_copy(momentum.at[rows], m.at[rows], local.at[2 * k + 1]),
            pltpu.make_async_copy(grad.at[rows], g.at[rows], local.at[2 * k + 2]),
        ]
        for copy in pair:
            copy.start()
        loads.append((rows, pair))
    net.barrier()
    own.wait()

    def add():
        for rows, pair in loads:
            for copy in pair:
                copy.wait()
            buffer[rows, :] = (m[rows, :].astype(F32) + g[rows, :].astype(F32)).astype(BF16)

    gather_all(net, block.at[y, c], out, add)


def left_kernel(dims, part, left, gram, rc, acc, ry, g, rgc, g1, rgy, g2, rgx, g3, gz, send, recv):
    net = Net(dims, send, recv)
    z, x, y, c = net.at
    net.barrier()
    copies = [net.start(part.at[:, t], rc.at[d], 3, t) for d, (t, _) in enumerate(net.peers(3))]
    for copy in copies:
        copy.wait()
    total = part[:, c]
    for d in range(len(copies)):
        total = total + rc[d]
    acc[...] = total
    copies = [net.start(acc.at[t], ry.at[d], 2, t) for d, (t, _) in enumerate(net.peers(2))]
    for copy in copies:
        copy.wait()
    own = acc[y]
    for d in range(len(copies)):
        own = own + ry[d]
    left[y, c] = own
    rows = [net.start(left.at[y, c], left.at[y, c], 2, t) for t, _ in net.peers(2)]
    product = lax.dot_general(own, own, (((0,), (0,)), ((), ())), precision=HIGHEST, preferred_element_type=F32)
    g[...] = product.reshape(g.shape)
    copies = [net.start(g.at[t], rgc.at[d], 3, t) for d, (t, _) in enumerate(net.peers(3))]
    for copy in copies:
        copy.wait()
    total = g[c]
    for d in range(len(copies)):
        total = total + rgc[d]
    g1[...] = total
    copies = [net.start(g1.at[t], rgy.at[d], 2, t) for d, (t, _) in enumerate(net.peers(2))]
    for copy in copies:
        copy.wait()
    total = g1[y]
    for d in range(len(copies)):
        total = total + rgy[d]
    g2[...] = total
    copies = [net.start(g2.at[t], rgx.at[d], 1, t) for d, (t, _) in enumerate(net.peers(1))]
    for copy in rows:
        copy.wait()
    rows = [net.start(left.at[:, c], left.at[:, c], 3, t) for t, _ in net.peers(3)]
    for copy in copies:
        copy.wait()
    total = g2[x]
    for d in range(len(copies)):
        total = total + rgx[d]
    g3[...] = total
    gz[z] = total
    copies = [net.start(g3, gz.at[z], 0, t) for t, _ in net.peers(0)]
    for copy in copies:
        copy.wait()
    total = gz[0]
    for d in range(1, dims[0]):
        total = total + gz[d]
    gram[c, y, x] = total
    for axis, view in ((1, gram.at[c, y, x]), (2, gram.at[c, y]), (3, gram.at[c])):
        copies = [net.start(view, view, axis, t) for t, _ in net.peers(axis)]
        for copy in copies:
            copy.wait()
    for copy in rows:
        copy.wait()


def factor_inverse(block):
    n = block.shape[0]
    row = lax.broadcasted_iota(jnp.int32, (8, n), 0)
    lane = lax.broadcasted_iota(jnp.int32, (8, n), 1)
    parts = [
        jnp.concatenate([block[8 * i : 8 * i + 8, :], jnp.where(lane == row + 8 * i, 1.0, 0.0).astype(F32)], axis=1)
        for i in range(n // 8)
    ]
    ids = lax.broadcasted_iota(jnp.int32, (8, 2 * n), 0)
    for j in range(0, n, PIVOTS):
        first, o = j // 8, j % 8
        head = parts[first]
        s = {}
        for p in range(PIVOTS):
            for q in range(p, PIVOTS):
                s[p, q] = jnp.broadcast_to(head[o + p : o + p + 1, j + q : j + q + 1], (1, 2 * n))
        rows = [head[o + p : o + p + 1, :] for p in range(PIVOTS)]
        cols = [
            [jnp.broadcast_to(part[:, j + p : j + p + 1], (8, 2 * n)) for part in parts[first:]]
            for p in range(PIVOTS)
        ]
        total = None
        done = []
        for p in range(PIVOTS):
            r = lax.rsqrt(s[p, p])
            inv = r * r
            for q in range(p + 1, PIVOTS):
                t = s[p, q] * inv
                rows[q] = rows[q] - t * rows[p]
                cols[q] = [cq - t * cp for cq, cp in zip(cols[q], cols[p])]
                for w in range(q, PIVOTS):
                    s[q, w] = s[q, w] - t * s[p, w]
            done.append(rows[p] * r)
            scaled = rows[p] * inv
            terms = [cp * scaled for cp in cols[p]]
            total = terms if total is None else [u + v for u, v in zip(total, terms)]
        head = jnp.where(ids >= o + PIVOTS, head - total[0], head)
        for p in range(PIVOTS):
            head = jnp.where(ids == o + p, done[p], head)
        rest = [part - u for part, u in zip(parts[first + 1 :], total[1:])]
        parts = parts[:first] + [head] + rest
    return jnp.concatenate(parts, axis=0)[:, n:]


def ortho_kernel(gram, left, ortho, rounded, work, inverse):
    n = gram.shape[0]
    row = lax.broadcasted_iota(jnp.int32, (n, n), 0)
    col = lax.broadcasted_iota(jnp.int32, (n, n), 1)
    work[:, :n] = gram[...]
    work[:, n:] = jnp.where(row == col, 1.0, 0.0).astype(F32)
    inverse[...] = jnp.zeros((n, n), F32)
    for lo in range(0, n, BLOCK):
        hi = lo + BLOCK
        start, end = hi // 128 * 128, (n + hi + 127) // 128 * 128
        corner = factor_inverse(work[lo:hi, lo:hi])
        upper = jnp.dot(corner, work[lo:hi, start:end], precision=HIGHEST, preferred_element_type=F32)
        inverse[lo:hi, : end - n] = upper[:, n - start :]
        if hi < n:
            work[hi:, start:end] -= lax.dot_general(
                upper[:, hi - start : n - start], upper, (((0,), (0,)), ((), ())),
                precision=HIGHEST, preferred_element_type=F32,
            )
    result = lax.dot_general(
        left[...], inverse[...], (((1,), (1,)), ((), ())), precision=HIGHEST, preferred_element_type=F32
    )
    ortho[...] = result
    rounded[...] = result.astype(BF16)


def right_kernel(dims, buffer, ortho, out, part, sc, rc, acc, sya, rya, sxb, rxb, a2, b2, sxa, rxa, syb, ryb, a3, sz, rz, own, send, recv):
    net = Net(dims, send, recv)
    nz, nx, ny, nc = dims
    z, x, y, c = net.at
    half = nz // 2
    a, b = slice(0, half), slice(half, nz)
    net.barrier()
    copies = []
    wide = buffer.shape[1] // nz
    for i in range(nz):
        product = lax.dot_general(
            buffer[:, i * wide : (i + 1) * wide], ortho[...], (((0,), (0,)), ((), ())), preferred_element_type=F32
        )
        part[i] = product.reshape(part.shape[1:])
        for d, (t, _) in enumerate(net.peers(3)):
            sc[d, i] = part[i, :, :, t].astype(BF16)
            copies.append(net.start(sc.at[d, i], rc.at[d, i], 3, t))
    for copy in copies:
        copy.wait()
    for i in range(nz):
        total = part[i, :, :, c]
        for d in range(nc - 1):
            total = total + rc[d, i].astype(F32)
        acc[i] = total
    copies = []
    for d, (t, _) in enumerate(net.peers(2)):
        sya[d] = acc[a, :, t].astype(BF16)
        copies.append(net.start(sya.at[d], rya.at[d], 2, t))
    for d, (t, _) in enumerate(net.peers(1)):
        sxb[d] = acc[b, t].astype(BF16)
        copies.append(net.start(sxb.at[d], rxb.at[d], 1, t))
    for copy in copies:
        copy.wait()
    total = acc[a, :, y]
    for d in range(ny - 1):
        total = total + rya[d].astype(F32)
    a2[...] = total
    total = acc[b, x]
    for d in range(nx - 1):
        total = total + rxb[d].astype(F32)
    b2[...] = total
    copies = []
    for d, (t, _) in enumerate(net.peers(1)):
        sxa[d] = a2[:, t].astype(BF16)
        copies.append(net.start(sxa.at[d], rxa.at[d], 1, t))
    for d, (t, _) in enumerate(net.peers(2)):
        syb[d] = b2[:, t].astype(BF16)
        copies.append(net.start(syb.at[d], ryb.at[d], 2, t))
    for copy in copies:
        copy.wait()
    total = a2[:, x]
    for d in range(nx - 1):
        total = total + rxa[d].astype(F32)
    a3[a] = total
    total = b2[:, y]
    for d in range(ny - 1):
        total = total + ryb[d].astype(F32)
    a3[b] = total
    copies = []
    for d, (t, _) in enumerate(net.peers(0)):
        sz[d] = a3[t].astype(BF16)
        copies.append(net.start(sz.at[d], rz.at[d], 0, t))
    for copy in copies:
        copy.wait()
    total = a3[z]
    for d in range(nz - 1):
        total = total + rz[d].astype(F32)
    mine = (total * (1.0 / (ny * nc))).astype(BF16)
    own[...] = mine
    out[z, x, y, c] = mine
    gather_all(net, own, out)


def call(kernel, dims, identity, operands, outs, scratch, local=0):
    vmem = pl.BlockSpec(memory_space=pltpu.VMEM)
    rest = pl.BlockSpec(memory_space=pltpu.MemorySpace.HBM)
    sems = [pltpu.SemaphoreType.DMA((MAX_COPIES,))] * 2
    if local:
        sems = sems + [pltpu.SemaphoreType.DMA((local,))]
    single = not isinstance(outs, tuple)
    return pl.pallas_call(
        functools.partial(kernel, dims),
        out_shape=outs,
        in_specs=[vmem] + [rest if local else vmem] * (len(operands) - 1),
        out_specs=vmem if single else (vmem,) * len(outs),
        scratch_shapes=[pltpu.VMEM(shape, kind) for shape, kind in scratch] + sems,
        compiler_params=pltpu.CompilerParams(
            collective_id=identity, has_side_effects=True, vmem_limit_bytes=48 << 20
        ),
    )(*operands)


def gather(dims, block, momentum, grad):
    nz, nx, ny, nc = dims
    rows, rank = block.shape
    piece = rows // (ny * nc)
    full, buffer_b = call(
        gather_kernel, dims, 0, (block.reshape(ny, nc, piece, rank), momentum, grad),
        (jax.ShapeDtypeStruct((nz, nx, ny, nc, piece, rank), BF16), jax.ShapeDtypeStruct(momentum.shape, BF16)),
        [(momentum.shape, BF16), (momentum.shape, BF16)], local=2 * CHUNKS + 1,
    )
    return full.reshape(rows * nz * nx, rank), buffer_b


def sum_left(dims, part):
    nz, nx, ny, nc = dims
    rows, rank = part.shape
    piece = rows // (ny * nc)
    g = rank // (nc * ny * nx)
    pc, py, px = max(nc - 1, 1), max(ny - 1, 1), max(nx - 1, 1)
    left, gram = call(
        left_kernel, dims, 1, (part.reshape(ny, nc, piece, rank),),
        (jax.ShapeDtypeStruct((ny, nc, piece, rank), F32), jax.ShapeDtypeStruct((nc, ny, nx, g, rank), F32)),
        [
            ((pc, ny, piece, rank), F32), ((ny, piece, rank), F32), ((py, piece, rank), F32),
            ((nc, ny, nx, g, rank), F32), ((pc, ny, nx, g, rank), F32), ((ny, nx, g, rank), F32),
            ((py, nx, g, rank), F32), ((nx, g, rank), F32), ((px, g, rank), F32), ((g, rank), F32),
            ((nz, g, rank), F32),
        ],
    )
    return left.reshape(rows, rank), gram.reshape(rank, rank)


def sum_right(dims, buffer_b, ortho_b):
    nz, nx, ny, nc = dims
    width, rank = buffer_b.shape[1], ortho_b.shape[1]
    piece = width // (nz * nx * ny * nc)
    low = nz // 2
    high = nz - low
    pc, py, px, pz = max(nc - 1, 1), max(ny - 1, 1), max(nx - 1, 1), max(nz - 1, 1)
    two = lambda shape, kind: [(shape, kind), (shape, kind)]
    full = call(
        right_kernel, dims, 2, (buffer_b, ortho_b),
        jax.ShapeDtypeStruct((nz, nx, ny, nc, piece, rank), BF16),
        [((nz, nx, ny, nc, piece, rank), F32)]
        + two((pc, nz, nx, ny, piece, rank), BF16)
        + [((nz, nx, ny, piece, rank), F32)]
        + two((py, low, nx, piece, rank), BF16)
        + two((px, high, ny, piece, rank), BF16)
        + [((low, nx, piece, rank), F32), ((high, ny, piece, rank), F32)]
        + two((px, low, piece, rank), BF16)
        + two((py, high, piece, rank), BF16)
        + [((nz, piece, rank), F32)]
        + two((pz, piece, rank), BF16)
        + [((piece, rank), BF16)],
    )
    return full.reshape(width, rank)


def orthonormal(gram, left):
    rank = gram.shape[0]
    vmem = pl.BlockSpec(memory_space=pltpu.VMEM)
    return pl.pallas_call(
        ortho_kernel,
        out_shape=(jax.ShapeDtypeStruct(left.shape, F32), jax.ShapeDtypeStruct(left.shape, BF16)),
        in_specs=[vmem, vmem],
        out_specs=(vmem, vmem),
        scratch_shapes=[pltpu.VMEM((rank, 2 * rank), F32), pltpu.VMEM((rank, rank), F32)],
        compiler_params=pltpu.CompilerParams(vmem_limit_bytes=32 << 20),
    )(gram, left)


def shards(dims, momentum, grad, right_prev):
    rows = grad.shape[2]
    width = grad.shape[3]
    rank = right_prev.shape[2]
    factor = width / math.sqrt(rank)
    buffer = momentum[0, 0].astype(F32) + grad[0, 0].astype(F32)
    prev_full, buffer_b = gather(dims, right_prev[0], momentum[0, 0], grad[0, 0])
    local_left = jnp.dot(buffer_b, prev_full, preferred_element_type=F32)
    summed, gram = sum_left(dims, local_left)
    ortho, ortho_b = orthonormal(gram, summed)
    right_full = sum_right(dims, buffer_b, ortho_b)
    wide = right_full.astype(F32)
    norms = jnp.sqrt(jnp.sum(wide * wide, axis=0) + epsilon_norm)
    right_own = lax.dynamic_slice_in_dim(right_full, lax.axis_index("shard") * rows, rows, axis=0)
    scaled = (ortho * (factor / norms)).astype(BF16)
    feedback = lax.dot_general(ortho_b, right_full, (((1,), (1,)), ((), ())), preferred_element_type=F32)
    momentum_new = (buffer - (1.0 - momentum_decay) * feedback).astype(BF16)
    stepped = lax.dot_general(scaled, right_full, (((1,), (1,)), ((), ())), preferred_element_type=F32)
    return momentum_new[None, None], stepped.astype(BF16)[None], right_own[None]


def solution(mesh):
    dims = grid_of(mesh.shape["shard"], mesh.shape["replica"])
    return jax.shard_map(
        functools.partial(shards, dims),
        mesh=mesh,
        in_specs=(
            P(None, "replica", "shard", None),
            P(None, "replica", "shard", None),
            P(None, "shard", None),
        ),
        out_specs=(
            P(None, "replica", "shard", None),
            P(None, "shard", None),
            P(None, "shard", None),
        ),
        check_vma=False,
    )
```

```python
import functools
import math

import jax
import jax.numpy as jnp
from jax import lax
from jax.experimental import pallas as pl
from jax.experimental.pallas import tpu as pltpu
from jax.sharding import PartitionSpec as P

momentum_decay = 0.95
epsilon_norm = 1e-06
MESH = pl.DeviceIdType.MESH
HIGHEST = lax.Precision.HIGHEST
F32 = jnp.float32
BF16 = jnp.bfloat16
BLOCK = 64
PIVOTS = 4
CHUNKS = 8


def grid_of(shards_n, replicas_n):
    x = math.isqrt(shards_n // 2)
    if x < 1 or 2 * x * x != shards_n:
        x = 1
    c = 2 if replicas_n % 2 == 0 else 1
    return shards_n // x, x, replicas_n // c, c


class Net:
    def __init__(self, dims, send, recv):
        self.dims = dims
        _, nx, _, nc = dims
        s = lax.axis_index("shard")
        r = lax.axis_index("replica")
        self.at = [s // nx, s % nx, r // nc, r % nc]
        self.send, self.recv, self.used = send, recv, 0

    def device(self, axis, coordinate):
        place = list(self.at)
        place[axis] = coordinate
        return {
            "shard": place[0] * self.dims[1] + place[1],
            "replica": place[2] * self.dims[3] + place[3],
        }

    def peers(self, axis):
        n, me = self.dims[axis], self.at[axis]
        distances = sorted(range(1, n), key=lambda d: (min(d, n - d), d))
        return [((me + d) % n, (me + n - d) % n) for d in distances]

    def barrier(self):
        sem = pltpu.get_barrier_semaphore()
        count = 0
        for axis in range(4):
            for target, _ in self.peers(axis):
                pl.semaphore_signal(sem, inc=1, device_id=self.device(axis, target), device_id_type=MESH)
                count += 1
        pl.semaphore_wait(sem, count)

    def start(self, src, dst, axis, target):
        i = self.used
        self.used += 1
        copy = pltpu.make_async_remote_copy(
            src_ref=src,
            dst_ref=dst,
            send_sem=self.send.at[i],
            recv_sem=self.recv.at[i],
            device_id=self.device(axis, target),
            device_id_type=MESH,
        )
        copy.start()
        return copy


def gather_all(net, own, out, work=None):
    z, x, y, c = net.at
    piece = out.shape[-2]
    a, b = pl.ds(0, piece // 2), pl.ds(piece // 2, piece - piece // 2)
    sent = []

    def pair(view):
        for t, _ in net.peers(3):
            sent.append(net.start(view, view, 3, t))

    def spread(i, src):
        dst = out.at[i, x, y, c]
        along_x = [(net.start(src, dst, 1, t), f) for t, f in net.peers(1)]
        along_y = [(net.start(src, dst, 2, t), f) for t, f in net.peers(2)]
        for t, _ in net.peers(3):
            sent.append(net.start(src, dst, 3, t))
        return i, along_x, along_y

    def relay(i, along_x, along_y):
        corner = []
        for copy, f in along_x:
            copy.wait()
            view = out.at[i, f, y, c, a]
            corner += [(net.start(view, view, 2, t), out.at[i, f, g, c, a]) for t, g in net.peers(2)]
            pair(out.at[i, f, y, c])
        for copy, f in along_y:
            copy.wait()
            view = out.at[i, x, f, c, b]
            corner += [(net.start(view, view, 1, t), out.at[i, g, f, c, b]) for t, g in net.peers(1)]
            pair(out.at[i, x, f, c])
        return corner

    along_z = [(net.start(own, out.at[z, x, y, c], 0, t), f) for t, f in net.peers(0)]
    first = spread(z, own)
    if work is not None:
        work()
    corners = relay(*first)
    waves = []
    for copy, f in along_z:
        copy.wait()
        waves.append(spread(f, out.at[f, x, y, c]))
    for wave in waves:
        corners += relay(*wave)
    for copy, view in corners:
        copy.wait()
        pair(view)
    for copy in sent:
        copy.wait()


def copies_of(dims):
    nz, nx, ny, nc = dims
    x, y, c = nx - 1, ny - 1, nc - 1
    gathered = (nz - 1) + nz * (x + y + c + x * (y + c) + y * (x + c) + 2 * x * y * c)
    summed = nz * (c + 2 * x * y + x + y + 1)
    return 2 * gathered + summed + 4 * c + 5 * y + 2 * x + nz + 8


def prefetch(momentum, grad, m, g, local):
    loads = []
    size = m.shape[0] // CHUNKS
    for k in range(CHUNKS):
        rows = pl.ds(k * size, size)
        pair = [
            pltpu.make_async_copy(momentum.at[rows], m.at[rows], local.at[2 * k + 1]),
            pltpu.make_async_copy(grad.at[rows], g.at[rows], local.at[2 * k + 2]),
        ]
        for copy in pair:
            copy.start()
        loads.append((rows, pair))
    return loads


def sum_left(net, part, left, gram, rc, acc, ry, g, rgc, g1, rgy, g2, rgx, g3, gz):
    z, x, y, c = net.at
    copies = [net.start(part.at[:, t], rc.at[d], 3, t) for d, (t, _) in enumerate(net.peers(3))]
    for copy in copies:
        copy.wait()
    total = part[:, c]
    for d in range(len(copies)):
        total = total + rc[d]
    acc[...] = total
    copies = [net.start(acc.at[t], ry.at[d], 2, t) for d, (t, _) in enumerate(net.peers(2))]
    for copy in copies:
        copy.wait()
    own = acc[y]
    for d in range(len(copies)):
        own = own + ry[d]
    left[y, c] = own
    rows = [net.start(left.at[y, c], left.at[y, c], 2, t) for t, _ in net.peers(2)]
    product = lax.dot_general(own, own, (((0,), (0,)), ((), ())), precision=HIGHEST, preferred_element_type=F32)
    g[...] = product.reshape(g.shape)
    copies = [net.start(g.at[t], rgc.at[d], 3, t) for d, (t, _) in enumerate(net.peers(3))]
    for copy in copies:
        copy.wait()
    total = g[c]
    for d in range(len(copies)):
        total = total + rgc[d]
    g1[...] = total
    copies = [net.start(g1.at[t], rgy.at[d], 2, t) for d, (t, _) in enumerate(net.peers(2))]
    for copy in copies:
        copy.wait()
    total = g1[y]
    for d in range(len(copies)):
        total = total + rgy[d]
    g2[...] = total
    copies = [net.start(g2.at[t], rgx.at[d], 1, t) for d, (t, _) in enumerate(net.peers(1))]
    for copy in rows:
        copy.wait()
    rows = [net.start(left.at[:, c], left.at[:, c], 3, t) for t, _ in net.peers(3)]
    for copy in copies:
        copy.wait()
    total = g2[x]
    for d in range(len(copies)):
        total = total + rgx[d]
    g3[...] = total
    gz[z] = total
    copies = [net.start(g3, gz.at[z], 0, t) for t, _ in net.peers(0)]
    for copy in copies:
        copy.wait()
    total = gz[0]
    for d in range(1, gz.shape[0]):
        total = total + gz[d]
    gram[c, y, x] = total
    for axis, view in ((1, gram.at[c, y, x]), (2, gram.at[c, y]), (3, gram.at[c])):
        copies = [net.start(view, view, axis, t) for t, _ in net.peers(axis)]
        for copy in copies:
            copy.wait()
    for copy in rows:
        copy.wait()


def factor_inverse(block):
    n = block.shape[0]
    row = lax.broadcasted_iota(jnp.int32, (8, n), 0)
    lane = lax.broadcasted_iota(jnp.int32, (8, n), 1)
    parts = [
        jnp.concatenate([block[8 * i : 8 * i + 8, :], jnp.where(lane == row + 8 * i, 1.0, 0.0).astype(F32)], axis=1)
        for i in range(n // 8)
    ]
    ids = lax.broadcasted_iota(jnp.int32, (8, 2 * n), 0)
    for j in range(0, n, PIVOTS):
        first, o = j // 8, j % 8
        head = parts[first]
        s = {}
        for p in range(PIVOTS):
            for q in range(p, PIVOTS):
                s[p, q] = jnp.broadcast_to(head[o + p : o + p + 1, j + q : j + q + 1], (1, 2 * n))
        rows = [head[o + p : o + p + 1, :] for p in range(PIVOTS)]
        cols = [
            [jnp.broadcast_to(part[:, j + p : j + p + 1], (8, 2 * n)) for part in parts[first:]]
            for p in range(PIVOTS)
        ]
        total = None
        done = []
        for p in range(PIVOTS):
            r = lax.rsqrt(s[p, p])
            inv = r * r
            for q in range(p + 1, PIVOTS):
                t = s[p, q] * inv
                rows[q] = rows[q] - t * rows[p]
                cols[q] = [cq - t * cp for cq, cp in zip(cols[q], cols[p])]
                for w in range(q, PIVOTS):
                    s[q, w] = s[q, w] - t * s[p, w]
            done.append(rows[p] * r)
            scaled = rows[p] * inv
            terms = [cp * scaled for cp in cols[p]]
            total = terms if total is None else [u + v for u, v in zip(total, terms)]
        head = jnp.where(ids >= o + PIVOTS, head - total[0], head)
        for p in range(PIVOTS):
            head = jnp.where(ids == o + p, done[p], head)
        rest = [part - u for part, u in zip(parts[first + 1 :], total[1:])]
        parts = parts[:first] + [head] + rest
    return jnp.concatenate(parts, axis=0)[:, n:]


def orthonormal(gram, left, ortho, rounded, work, inverse):
    n = gram.shape[-1]
    row = lax.broadcasted_iota(jnp.int32, (n, n), 0)
    col = lax.broadcasted_iota(jnp.int32, (n, n), 1)
    work[:, :n] = gram[...].reshape(n, n)
    work[:, n:] = jnp.where(row == col, 1.0, 0.0).astype(F32)
    inverse[...] = jnp.zeros((n, n), F32)
    for lo in range(0, n, BLOCK):
        hi = lo + BLOCK
        start, end = hi // 128 * 128, (n + hi + 127) // 128 * 128
        corner = factor_inverse(work[lo:hi, lo:hi])
        upper = jnp.dot(corner, work[lo:hi, start:end], precision=HIGHEST, preferred_element_type=F32)
        inverse[lo:hi, : end - n] = upper[:, n - start :]
        if hi < n:
            work[hi:, start:end] -= lax.dot_general(
                upper[:, hi - start : n - start], upper, (((0,), (0,)), ((), ())),
                precision=HIGHEST, preferred_element_type=F32,
            )
    result = lax.dot_general(
        left[...].reshape(ortho.shape), inverse[...], (((1,), (1,)), ((), ())), precision=HIGHEST, preferred_element_type=F32
    )
    ortho[...] = result
    rounded[...] = result.astype(BF16)


def sum_right(net, buffer, ortho, out, part, sc, rc, acc, sa, ra, sb, rb, sx, rx, sy, ry, sz, rz, own):
    nz, nx, ny, nc = net.dims
    z, x, y, c = net.at
    xs, ys, cs = net.peers(1), net.peers(2), net.peers(3)
    targets = [t for t, _ in reversed(net.peers(0))] + [z]
    half = acc.shape[-2] // 2
    wide = buffer.shape[1] // nz
    corners = [(i, j) for j in range(ny - 1) for i in range(nx - 1)]
    pending = {}

    def multiply(k):
        columns = pl.ds(pl.multiple_of(targets[k] * wide, 128), wide)
        product = lax.dot_general(
            buffer[:, columns], ortho[...], (((0,), (0,)), ((), ())), preferred_element_type=F32
        )
        part[k] = product.reshape(part.shape[1:])
        copies = []
        for d, (t, _) in enumerate(cs):
            sc[d, k] = part[k, :, :, t].astype(BF16)
            copies.append(net.start(sc.at[d, k], rc.at[d, k], 3, t))
        pending[k] = copies

    def corner(k):
        for copy in pending[k]:
            copy.wait()
        total = part[k, :, :, c]
        for d in range(nc - 1):
            total = total + rc[d, k].astype(F32)
        acc[k] = total
        copies = []
        for e, (i, j) in enumerate(corners):
            tx, ty = xs[i][0], ys[j][0]
            sa[e, k] = acc[k, tx, ty, :half].astype(BF16)
            copies.append(net.start(sa.at[e, k], ra.at[e, k], 2, ty))
            sb[e, k] = acc[k, tx, ty, half:].astype(BF16)
            copies.append(net.start(sb.at[e, k], rb.at[e, k], 1, tx))
        pending[k] = copies

    def across(k):
        for copy in pending[k]:
            copy.wait()
        copies = []
        for i, (tx, _) in enumerate(xs):
            low = acc[k, tx, y, :half]
            for e, (p, _) in enumerate(corners):
                if p == i:
                    low = low + ra[e, k].astype(F32)
            sx[i, k, :half] = low.astype(BF16)
            sx[i, k, half:] = acc[k, tx, y, half:].astype(BF16)
            copies.append(net.start(sx.at[i, k], rx.at[i, k], 1, tx))
        for j, (ty, _) in enumerate(ys):
            high = acc[k, x, ty, half:]
            for e, (_, q) in enumerate(corners):
                if q == j:
                    high = high + rb[e, k].astype(F32)
            sy[j, k, :half] = acc[k, x, ty, :half].astype(BF16)
            sy[j, k, half:] = high.astype(BF16)
            copies.append(net.start(sy.at[j, k], ry.at[j, k], 2, ty))
        pending[k] = copies

    def along(k):
        for copy in pending[k]:
            copy.wait()
        total = acc[k, x, y]
        for i in range(nx - 1):
            total = total + rx[i, k].astype(F32)
        for j in range(ny - 1):
            total = total + ry[j, k].astype(F32)
        if k == nz - 1:
            return total
        sz[k] = total.astype(BF16)
        pending[k] = [net.start(sz.at[k], rz.at[k], 0, targets[k])]
        return None

    total = None
    for step in range(nz + 3):
        for lag, phase in ((3, along), (2, across), (1, corner), (0, multiply)):
            if 0 <= step - lag < nz:
                total = phase(step - lag)
                if lag == 3:
                    final = total
    for k in range(nz - 1):
        for copy in pending[k]:
            copy.wait()
        final = final + rz[k].astype(F32)
    mine = (final * (1.0 / (ny * nc))).astype(BF16)
    own[...] = mine
    out[z, x, y, c] = mine
    gather_all(net, own, out)


def kernel(dims, block, momentum, grad, right, ortho, rounded, prev, buffer, m, g, part, left, gram, *rest):
    lefts, (work, inverse), rights = rest[:11], rest[11:13], rest[13:-3]
    send, recv, local = rest[-3:]
    net = Net(dims, send, recv)
    z, x, y, c = net.at
    own = pltpu.make_async_copy(block.at[y, c], prev.at[z, x, y, c], local.at[0])
    own.start()
    loads = prefetch(momentum, grad, m, g, local)
    net.barrier()
    own.wait()

    def add():
        for rows, pair in loads:
            for copy in pair:
                copy.wait()
            buffer[rows, :] = (m[rows, :].astype(F32) + g[rows, :].astype(F32)).astype(BF16)

    gather_all(net, block.at[y, c], prev, add)
    width = buffer.shape[1]
    product = jnp.dot(buffer[...], prev[...].reshape(width, prev.shape[-1]), preferred_element_type=F32)
    part[...] = product.reshape(part.shape)
    sum_left(net, part, left, gram, *lefts)
    orthonormal(gram, left, ortho, rounded, work, inverse)
    sum_right(net, buffer, rounded, right, *rights)


def factors(dims, block, momentum, grad):
    nz, nx, ny, nc = dims
    rows, rank = block.shape
    width = momentum.shape[1]
    lp = rows // (ny * nc)
    rp = width // (nz * nx * ny * nc)
    gr = rank // (nc * ny * nx)
    pc, py, px, pz = max(nc - 1, 1), max(ny - 1, 1), max(nx - 1, 1), max(nz - 1, 1)
    pe, half = px * py, rp // 2
    full = (nz, nx, ny, nc, rp, rank)
    scratch = [
        ((nz, nx, ny, nc, lp, rank), BF16), (momentum.shape, BF16), (momentum.shape, BF16), (momentum.shape, BF16),
        ((ny, nc, lp, rank), F32), ((ny, nc, lp, rank), F32), ((nc, ny, nx, gr, rank), F32),
        ((pc, ny, lp, rank), F32), ((ny, lp, rank), F32), ((py, lp, rank), F32),
        ((nc, ny, nx, gr, rank), F32), ((pc, ny, nx, gr, rank), F32), ((ny, nx, gr, rank), F32),
        ((py, nx, gr, rank), F32), ((nx, gr, rank), F32), ((px, gr, rank), F32), ((gr, rank), F32),
        ((nz, gr, rank), F32),
        ((rank, 2 * rank), F32), ((rank, rank), F32),
        (full, F32),
        ((pc, nz, nx, ny, rp, rank), BF16), ((pc, nz, nx, ny, rp, rank), BF16),
        ((nz, nx, ny, rp, rank), F32),
        ((pe, nz, half, rank), BF16), ((pe, nz, half, rank), BF16),
        ((pe, nz, rp - half, rank), BF16), ((pe, nz, rp - half, rank), BF16),
        ((px, nz, rp, rank), BF16), ((px, nz, rp, rank), BF16),
        ((py, nz, rp, rank), BF16), ((py, nz, rp, rank), BF16),
        ((pz, rp, rank), BF16), ((pz, rp, rank), BF16),
        ((rp, rank), BF16),
    ]
    copies = copies_of(dims)
    vmem = pl.BlockSpec(memory_space=pltpu.VMEM)
    hbm = pl.BlockSpec(memory_space=pltpu.MemorySpace.HBM)
    right, ortho, rounded = pl.pallas_call(
        functools.partial(kernel, dims),
        out_shape=(
            jax.ShapeDtypeStruct(full, BF16),
            jax.ShapeDtypeStruct((rows, rank), F32),
            jax.ShapeDtypeStruct((rows, rank), BF16),
        ),
        in_specs=[vmem, hbm, hbm],
        out_specs=(vmem, vmem, vmem),
        scratch_shapes=[pltpu.VMEM(shape, kind) for shape, kind in scratch]
        + [pltpu.SemaphoreType.DMA((copies,))] * 2
        + [pltpu.SemaphoreType.DMA((2 * CHUNKS + 1,))],
        compiler_params=pltpu.CompilerParams(
            collective_id=0, has_side_effects=True, vmem_limit_bytes=50 << 20
        ),
    )(block.reshape(ny, nc, lp, rank), momentum, grad)
    return right.reshape(width, rank), ortho, rounded


def shards(dims, momentum, grad, right_prev):
    rows = grad.shape[2]
    width = grad.shape[3]
    rank = right_prev.shape[2]
    factor = width / math.sqrt(rank)
    buffer = momentum[0, 0].astype(F32) + grad[0, 0].astype(F32)
    right_full, ortho, ortho_b = factors(dims, right_prev[0], momentum[0, 0], grad[0, 0])
    wide = right_full.astype(F32)
    norms = jnp.sqrt(jnp.sum(wide * wide, axis=0) + epsilon_norm)
    right_own = lax.dynamic_slice_in_dim(right_full, lax.axis_index("shard") * rows, rows, axis=0)
    scaled = (ortho * (factor / norms)).astype(BF16)
    feedback = lax.dot_general(ortho_b, right_full, (((1,), (1,)), ((), ())), preferred_element_type=F32)
    momentum_new = (buffer - (1.0 - momentum_decay) * feedback).astype(BF16)
    stepped = lax.dot_general(scaled, right_full, (((1,), (1,)), ((), ())), preferred_element_type=F32)
    return momentum_new[None, None], stepped.astype(BF16)[None], right_own[None]


def solution(mesh):
    dims = grid_of(mesh.shape["shard"], mesh.shape["replica"])
    return jax.shard_map(
        functools.partial(shards, dims),
        mesh=mesh,
        in_specs=(
            P(None, "replica", "shard", None),
            P(None, "replica", "shard", None),
            P(None, "shard", None),
        ),
        out_specs=(
            P(None, "replica", "shard", None),
            P(None, "shard", None),
            P(None, "shard", None),
        ),
        check_vma=False,
    )
```

```python
import functools
import math

import jax
import jax.numpy as jnp
from jax import lax
from jax.experimental import pallas as pl
from jax.experimental.pallas import tpu as pltpu
from jax.sharding import PartitionSpec as P

momentum_decay = 0.95
epsilon_norm = 1e-06
MESH = pl.DeviceIdType.MESH
HIGHEST = lax.Precision.HIGHEST
F32 = jnp.float32
BF16 = jnp.bfloat16
BLOCK = 64
PIVOTS = 4
CHUNKS = 8
TILES = 8


def grid_of(shards_n, replicas_n):
    x = math.isqrt(shards_n // 2)
    if x < 1 or 2 * x * x != shards_n:
        x = 1
    c = 2 if replicas_n % 2 == 0 else 1
    return shards_n // x, x, replicas_n // c, c


class Net:
    def __init__(self, dims, send, recv):
        self.dims = dims
        _, nx, _, nc = dims
        s = lax.axis_index("shard")
        r = lax.axis_index("replica")
        self.at = [s // nx, s % nx, r // nc, r % nc]
        self.send, self.recv, self.used = send, recv, 0

    def device(self, axis, coordinate):
        place = list(self.at)
        if axis is None:
            place[1], place[2] = coordinate
        else:
            place[axis] = coordinate
        return {
            "shard": place[0] * self.dims[1] + place[1],
            "replica": place[2] * self.dims[3] + place[3],
        }

    def peers(self, axis):
        n, me = self.dims[axis], self.at[axis]
        distances = sorted(range(1, n), key=lambda d: (min(d, n - d), d))
        return [((me + d) % n, (me + n - d) % n) for d in distances]

    def plane(self):
        nx, ny = self.dims[1:3]
        x, y = self.at[1:3]
        steps = sorted(((i, j) for i in range(nx) for j in range(ny) if i or j), key=lambda p: (min(p[0], nx - p[0]) + min(p[1], ny - p[1]), p))
        return [
            (((x + i) % nx, (y + j) % ny), ((x + nx - i) % nx, (y + ny - j) % ny)) for i, j in steps
        ]

    def barrier(self):
        sem = pltpu.get_barrier_semaphore()
        count = 0
        for axis in range(4):
            for target, _ in self.peers(axis):
                pl.semaphore_signal(sem, inc=1, device_id=self.device(axis, target), device_id_type=MESH)
                count += 1
        for target, _ in self.plane():
            pl.semaphore_signal(sem, inc=1, device_id=self.device(None, target), device_id_type=MESH)
            count += 1
        pl.semaphore_wait(sem, count)

    def start(self, src, dst, axis, target):
        i = self.used
        self.used += 1
        copy = pltpu.make_async_remote_copy(
            src_ref=src,
            dst_ref=dst,
            send_sem=self.send.at[i],
            recv_sem=self.recv.at[i],
            device_id=self.device(axis, target),
            device_id_type=MESH,
        )
        copy.start()
        return copy


def gather_all(net, own, out, work=None, use=None):
    z, x, y, c = net.at
    piece = out.shape[-2]
    a, b = pl.ds(0, piece // 2), pl.ds(piece // 2, piece - piece // 2)

    def pair(view, sent):
        for t, _ in net.peers(3):
            sent.append(net.start(view, view, 3, t))

    def spread(i, src):
        dst = out.at[i, x, y, c]
        along_x = [(net.start(src, dst, 1, t), f) for t, f in net.peers(1)]
        along_y = [(net.start(src, dst, 2, t), f) for t, f in net.peers(2)]
        sent = [net.start(src, dst, 3, t) for t, _ in net.peers(3)]
        return i, along_x, along_y, sent

    def relay(i, along_x, along_y, sent):
        corner = []
        for copy, f in along_x:
            copy.wait()
            view = out.at[i, f, y, c, a]
            corner += [(net.start(view, view, 2, t), out.at[i, f, g, c, a]) for t, g in net.peers(2)]
            pair(out.at[i, f, y, c], sent)
        for copy, f in along_y:
            copy.wait()
            view = out.at[i, x, f, c, b]
            corner += [(net.start(view, view, 1, t), out.at[i, g, f, c, b]) for t, g in net.peers(1)]
            pair(out.at[i, x, f, c], sent)
        return i, corner, sent

    along_z = [(net.start(own, out.at[z, x, y, c], 0, t), f) for t, f in net.peers(0)]
    first = spread(z, own)
    if work is not None:
        work()
    relayed = [relay(*first)]
    waves = []
    for copy, f in along_z:
        copy.wait()
        waves.append(spread(f, out.at[f, x, y, c]))
    relayed += [relay(*wave) for wave in waves]
    for i, corner, sent in relayed:
        for copy, view in corner:
            copy.wait()
            pair(view, sent)
    for i, corner, sent in relayed:
        for copy in sent:
            copy.wait()
        if use is not None:
            use(i)


def copies_of(dims):
    nz, nx, ny, nc = dims
    x, y, c = nx - 1, ny - 1, nc - 1
    gathered = (nz - 1) + nz * (x + y + c + x * (y + c) + y * (x + c) + 2 * x * y * c)
    summed = nz * (c + 2 * x * y + x + y + 1)
    return 2 * gathered + summed + 4 * c + 3 * y + 2 * nx * ny + nz + 8


def prefetch(momentum, grad, m, g, local):
    loads = []
    size = m.shape[0] // CHUNKS
    for k in range(CHUNKS):
        rows = pl.ds(k * size, size)
        pair = [
            pltpu.make_async_copy(momentum.at[rows], m.at[rows], local.at[2 * k + 1]),
            pltpu.make_async_copy(grad.at[rows], g.at[rows], local.at[2 * k + 2]),
        ]
        for copy in pair:
            copy.start()
        loads.append((rows, pair))
    return loads


def sum_left(net, part, left, gram, rc, acc, ry, g, rgc, g1, rg, g3, gz):
    z, x, y, c = net.at
    copies = [net.start(part.at[:, t], rc.at[d], 3, t) for d, (t, _) in enumerate(net.peers(3))]
    for copy in copies:
        copy.wait()
    total = part[:, c]
    for d in range(len(copies)):
        total = total + rc[d]
    acc[...] = total
    copies = [net.start(acc.at[t], ry.at[d], 2, t) for d, (t, _) in enumerate(net.peers(2))]
    for copy in copies:
        copy.wait()
    own = acc[y]
    for d in range(len(copies)):
        own = own + ry[d]
    left[y, c] = own
    rows = [net.start(left.at[y, c], left.at[y, c], 2, t) for t, _ in net.peers(2)]
    product = lax.dot_general(own, own, (((0,), (0,)), ((), ())), precision=HIGHEST, preferred_element_type=F32)
    g[...] = product.reshape(g.shape)
    copies = [net.start(g.at[t], rgc.at[d], 3, t) for d, (t, _) in enumerate(net.peers(3))]
    for copy in copies:
        copy.wait()
    total = g[c]
    for d in range(len(copies)):
        total = total + rgc[d]
    g1[...] = total
    copies = [net.start(g1.at[t[1], t[0]], rg.at[e], None, t) for e, (t, _) in enumerate(net.plane())]
    for copy in rows:
        copy.wait()
    rows = [net.start(left.at[:, c], left.at[:, c], 3, t) for t, _ in net.peers(3)]
    for copy in copies:
        copy.wait()
    total = g1[y, x]
    for e in range(len(copies)):
        total = total + rg[e]
    g3[...] = total
    gz[z] = total
    copies = [net.start(g3, gz.at[z], 0, t) for t, _ in net.peers(0)]
    for copy in copies:
        copy.wait()
    total = gz[0]
    for d in range(1, gz.shape[0]):
        total = total + gz[d]
    gram[c, y, x] = total
    view = gram.at[c, y, x]
    copies = [net.start(view, view, None, t) for t, _ in net.plane()]
    for copy in copies:
        copy.wait()
    copies = [net.start(gram.at[c], gram.at[c], 3, t) for t, _ in net.peers(3)]
    for copy in copies + rows:
        copy.wait()


def factor_inverse(block):
    n = block.shape[0]
    row = lax.broadcasted_iota(jnp.int32, (8, n), 0)
    lane = lax.broadcasted_iota(jnp.int32, (8, n), 1)
    parts = [
        jnp.concatenate([block[8 * i : 8 * i + 8, :], jnp.where(lane == row + 8 * i, 1.0, 0.0).astype(F32)], axis=1)
        for i in range(n // 8)
    ]
    ids = lax.broadcasted_iota(jnp.int32, (8, 2 * n), 0)
    for j in range(0, n, PIVOTS):
        first, o = j // 8, j % 8
        head = parts[first]
        s = {}
        for p in range(PIVOTS):
            for q in range(p, PIVOTS):
                s[p, q] = jnp.broadcast_to(head[o + p : o + p + 1, j + q : j + q + 1], (1, 2 * n))
        rows = [head[o + p : o + p + 1, :] for p in range(PIVOTS)]
        cols = [
            [jnp.broadcast_to(part[:, j + p : j + p + 1], (8, 2 * n)) for part in parts[first:]]
            for p in range(PIVOTS)
        ]
        total = None
        done = []
        for p in range(PIVOTS):
            r = lax.rsqrt(s[p, p])
            inv = r * r
            for q in range(p + 1, PIVOTS):
                t = s[p, q] * inv
                rows[q] = rows[q] - t * rows[p]
                cols[q] = [cq - t * cp for cq, cp in zip(cols[q], cols[p])]
                for w in range(q, PIVOTS):
                    s[q, w] = s[q, w] - t * s[p, w]
            done.append(rows[p] * r)
            scaled = rows[p] * inv
            terms = [cp * scaled for cp in cols[p]]
            total = terms if total is None else [u + v for u, v in zip(total, terms)]
        head = jnp.where(ids >= o + PIVOTS, head - total[0], head)
        for p in range(PIVOTS):
            head = jnp.where(ids == o + p, done[p], head)
        rest = [part - u for part, u in zip(parts[first + 1 :], total[1:])]
        parts = parts[:first] + [head] + rest
    return jnp.concatenate(parts, axis=0)[:, n:]


def orthonormal(gram, left, ortho, rounded, work, inverse):
    n = gram.shape[-1]
    row = lax.broadcasted_iota(jnp.int32, (n, n), 0)
    col = lax.broadcasted_iota(jnp.int32, (n, n), 1)
    work[:, :n] = gram[...].reshape(n, n)
    work[:, n:] = jnp.where(row == col, 1.0, 0.0).astype(F32)
    inverse[...] = jnp.zeros((n, n), F32)
    for lo in range(0, n, BLOCK):
        hi = lo + BLOCK
        start, end = hi // 128 * 128, (n + hi + 127) // 128 * 128
        corner = factor_inverse(work[lo:hi, lo:hi])
        upper = jnp.dot(corner, work[lo:hi, start:end], precision=HIGHEST, preferred_element_type=F32)
        inverse[lo:hi, : end - n] = upper[:, n - start :]
        if hi < n:
            work[hi:, start:end] -= lax.dot_general(
                upper[:, hi - start : n - start], upper, (((0,), (0,)), ((), ())),
                precision=HIGHEST, preferred_element_type=F32,
            )
    result = lax.dot_general(
        left[...].reshape(ortho.shape), inverse[...], (((1,), (1,)), ((), ())), precision=HIGHEST, preferred_element_type=F32
    )
    ortho[...] = result
    rounded[...] = result.astype(BF16)


def sum_right(net, use, buffer, ortho, out, part, sc, rc, acc, sa, ra, sb, rb, sx, rx, sy, ry, sz, rz, own):
    nz, nx, ny, nc = net.dims
    z, x, y, c = net.at
    xs, ys, cs = net.peers(1), net.peers(2), net.peers(3)
    targets = [t for t, _ in reversed(net.peers(0))] + [z]
    half = acc.shape[-2] // 2
    wide = buffer.shape[1] // nz
    corners = [(i, j) for j in range(ny - 1) for i in range(nx - 1)]
    pending = {}

    def multiply(k):
        columns = pl.ds(pl.multiple_of(targets[k] * wide, 128), wide)
        product = lax.dot_general(
            buffer[:, columns], ortho[...], (((0,), (0,)), ((), ())), preferred_element_type=F32
        )
        part[k] = product.reshape(part.shape[1:])
        copies = []
        for d, (t, _) in enumerate(cs):
            sc[d, k] = part[k, :, :, t].astype(BF16)
            copies.append(net.start(sc.at[d, k], rc.at[d, k], 3, t))
        pending[k] = copies

    def corner(k):
        for copy in pending[k]:
            copy.wait()
        total = part[k, :, :, c]
        for d in range(nc - 1):
            total = total + rc[d, k].astype(F32)
        acc[k] = total
        copies = []
        for e, (i, j) in enumerate(corners):
            tx, ty = xs[i][0], ys[j][0]
            sa[e, k] = acc[k, tx, ty, :half].astype(BF16)
            copies.append(net.start(sa.at[e, k], ra.at[e, k], 2, ty))
            sb[e, k] = acc[k, tx, ty, half:].astype(BF16)
            copies.append(net.start(sb.at[e, k], rb.at[e, k], 1, tx))
        pending[k] = copies

    def across(k):
        for copy in pending[k]:
            copy.wait()
        copies = []
        for i, (tx, _) in enumerate(xs):
            low = acc[k, tx, y, :half]
            for e, (p, _) in enumerate(corners):
                if p == i:
                    low = low + ra[e, k].astype(F32)
            sx[i, k, :half] = low.astype(BF16)
            sx[i, k, half:] = acc[k, tx, y, half:].astype(BF16)
            copies.append(net.start(sx.at[i, k], rx.at[i, k], 1, tx))
        for j, (ty, _) in enumerate(ys):
            high = acc[k, x, ty, half:]
            for e, (_, q) in enumerate(corners):
                if q == j:
                    high = high + rb[e, k].astype(F32)
            sy[j, k, :half] = acc[k, x, ty, :half].astype(BF16)
            sy[j, k, half:] = high.astype(BF16)
            copies.append(net.start(sy.at[j, k], ry.at[j, k], 2, ty))
        pending[k] = copies

    def along(k):
        for copy in pending[k]:
            copy.wait()
        total = acc[k, x, y]
        for i in range(nx - 1):
            total = total + rx[i, k].astype(F32)
        for j in range(ny - 1):
            total = total + ry[j, k].astype(F32)
        if k == nz - 1:
            return total
        sz[k] = total.astype(BF16)
        pending[k] = [net.start(sz.at[k], rz.at[k], 0, targets[k])]
        return None

    total = None
    for step in range(nz + 3):
        for lag, phase in ((3, along), (2, across), (1, corner), (0, multiply)):
            if 0 <= step - lag < nz:
                total = phase(step - lag)
                if lag == 3:
                    final = total
    for k in range(nz - 1):
        for copy in pending[k]:
            copy.wait()
        final = final + rz[k].astype(F32)
    mine = (final * (1.0 / (ny * nc))).astype(BF16)
    own[...] = mine
    out[z, x, y, c] = mine
    gather_all(net, own, out, use=use)


def kernel(dims, block, momentum, grad, right, ortho, rounded, moved, squares, prev, buffer, m, g, part, left, gram, *rest):
    lefts, (work, inverse), rights = rest[:9], rest[9:11], rest[11:-3]
    send, recv, local = rest[-3:]
    net = Net(dims, send, recv)
    z, x, y, c = net.at
    own = pltpu.make_async_copy(block.at[y, c], prev.at[z, x, y, c], local.at[0])
    own.start()
    loads = prefetch(momentum, grad, m, g, local)
    net.barrier()
    own.wait()

    def add():
        for rows, pair in loads:
            for copy in pair:
                copy.wait()
            buffer[rows, :] = (m[rows, :].astype(F32) + g[rows, :].astype(F32)).astype(BF16)

    gather_all(net, block.at[y, c], prev, add)
    width = buffer.shape[1]
    product = jnp.dot(buffer[...], prev[...].reshape(width, prev.shape[-1]), preferred_element_type=F32)
    part[...] = product.reshape(part.shape)
    sum_left(net, part, left, gram, *lefts)
    orthonormal(gram, left, ortho, rounded, work, inverse)
    squares[...] = jnp.zeros(squares.shape, F32)
    wide = width // dims[0]
    size = min(wide, 512)

    def use(i):
        rows = right[i].reshape(wide, right.shape[-1])
        square = rows.astype(F32)
        squares[0:1] = squares[0:1] + jnp.sum(square * square, axis=0, keepdims=True)
        for k in range(0, wide, size):
            columns = pl.ds(pl.multiple_of(i * wide + k, 128), size)
            feedback = lax.dot_general(
                rounded[...], rows[k : k + size], (((1,), (1,)), ((), ())), preferred_element_type=F32
            )
            total = m[:, columns].astype(F32) + g[:, columns].astype(F32)
            moved[:, columns] = (total - (1.0 - momentum_decay) * feedback).astype(BF16)

    sum_right(net, use, buffer, rounded, right, *rights)


def finish_kernel(factor, right, ortho, moved, squares, momentum_new, update, own, stage, sem):
    rows, rank = ortho.shape
    width = right.shape[0]
    first = pltpu.make_async_copy(moved, momentum_new, sem.at[0])
    first.start()
    start = pl.multiple_of(lax.axis_index("shard") * rows, rows)
    second = pltpu.make_async_copy(right.at[pl.ds(start, rows)], own, sem.at[1])
    second.start()
    norms = jnp.sqrt(squares[0:1, :] + epsilon_norm)
    scaled = (ortho[...] * (factor / norms)).astype(BF16)
    size = width // TILES
    copies = [first, second]
    for k in range(TILES):
        columns = slice(k * size, (k + 1) * size)
        stage[k] = lax.dot_general(
            scaled, right[columns, :], (((1,), (1,)), ((), ())), preferred_element_type=F32
        ).astype(BF16)
        copy = pltpu.make_async_copy(stage.at[k], update.at[:, columns], sem.at[2 + k])
        copy.start()
        copies.append(copy)
    for copy in copies:
        copy.wait()


def finish(right, ortho, moved, squares):
    width, rank = right.shape
    rows = ortho.shape[0]
    vmem = pl.BlockSpec(memory_space=pltpu.VMEM)
    hbm = pl.BlockSpec(memory_space=pltpu.MemorySpace.HBM)
    return pl.pallas_call(
        functools.partial(finish_kernel, width / math.sqrt(rank)),
        out_shape=(
            jax.ShapeDtypeStruct(moved.shape, BF16),
            jax.ShapeDtypeStruct(moved.shape, BF16),
            jax.ShapeDtypeStruct((rows, rank), BF16),
        ),
        in_specs=[vmem] * 4,
        out_specs=(hbm, hbm, hbm),
        scratch_shapes=[
            pltpu.VMEM((TILES, rows, width // TILES), BF16),
            pltpu.SemaphoreType.DMA((2 + TILES,)),
        ],
        compiler_params=pltpu.CompilerParams(vmem_limit_bytes=12 << 20),
    )(right, ortho, moved, squares)


def factors(dims, block, momentum, grad):
    nz, nx, ny, nc = dims
    rows, rank = block.shape
    width = momentum.shape[1]
    lp = rows // (ny * nc)
    rp = width // (nz * nx * ny * nc)
    gr = rank // (nc * ny * nx)
    pc, py, px, pz = max(nc - 1, 1), max(ny - 1, 1), max(nx - 1, 1), max(nz - 1, 1)
    pe, half = px * py, rp // 2
    full = (nz, nx, ny, nc, rp, rank)
    scratch = [
        ((nz, nx, ny, nc, lp, rank), BF16), (momentum.shape, BF16), (momentum.shape, BF16), (momentum.shape, BF16),
        ((ny, nc, lp, rank), F32), ((ny, nc, lp, rank), F32), ((nc, ny, nx, gr, rank), F32),
        ((pc, ny, lp, rank), F32), ((ny, lp, rank), F32), ((py, lp, rank), F32),
        ((nc, ny, nx, gr, rank), F32), ((pc, ny, nx, gr, rank), F32), ((ny, nx, gr, rank), F32),
        ((max(nx * ny - 1, 1), gr, rank), F32), ((gr, rank), F32),
        ((nz, gr, rank), F32),
        ((rank, 2 * rank), F32), ((rank, rank), F32),
        (full, F32),
        ((pc, nz, nx, ny, rp, rank), BF16), ((pc, nz, nx, ny, rp, rank), BF16),
        ((nz, nx, ny, rp, rank), F32),
        ((pe, nz, half, rank), BF16), ((pe, nz, half, rank), BF16),
        ((pe, nz, rp - half, rank), BF16), ((pe, nz, rp - half, rank), BF16),
        ((px, nz, rp, rank), BF16), ((px, nz, rp, rank), BF16),
        ((py, nz, rp, rank), BF16), ((py, nz, rp, rank), BF16),
        ((pz, rp, rank), BF16), ((pz, rp, rank), BF16),
        ((rp, rank), BF16),
    ]
    copies = copies_of(dims)
    vmem = pl.BlockSpec(memory_space=pltpu.VMEM)
    hbm = pl.BlockSpec(memory_space=pltpu.MemorySpace.HBM)
    right, ortho, _, moved, squares = pl.pallas_call(
        functools.partial(kernel, dims),
        out_shape=(
            jax.ShapeDtypeStruct(full, BF16),
            jax.ShapeDtypeStruct((rows, rank), F32),
            jax.ShapeDtypeStruct((rows, rank), BF16),
            jax.ShapeDtypeStruct(momentum.shape, BF16),
            jax.ShapeDtypeStruct((8, rank), F32),
        ),
        in_specs=[vmem, hbm, hbm],
        out_specs=(vmem,) * 5,
        scratch_shapes=[pltpu.VMEM(shape, kind) for shape, kind in scratch]
        + [pltpu.SemaphoreType.DMA((copies,))] * 2
        + [pltpu.SemaphoreType.DMA((2 * CHUNKS + 1,))],
        compiler_params=pltpu.CompilerParams(
            collective_id=0, has_side_effects=True, vmem_limit_bytes=36 << 20
        ),
    )(block.reshape(ny, nc, lp, rank), momentum, grad)
    return right.reshape(width, rank), ortho, moved, squares


def shards(dims, momentum, grad, right_prev):
    right, ortho, moved, squares = factors(dims, right_prev[0], momentum[0, 0], grad[0, 0])
    momentum_new, update, right_own = finish(right, ortho, moved, squares)
    return momentum_new[None, None], update[None], right_own[None]


def solution(mesh):
    dims = grid_of(mesh.shape["shard"], mesh.shape["replica"])
    return jax.shard_map(
        functools.partial(shards, dims),
        mesh=mesh,
        in_specs=(
            P(None, "replica", "shard", None),
            P(None, "replica", "shard", None),
            P(None, "shard", None),
        ),
        out_specs=(
            P(None, "replica", "shard", None),
            P(None, "shard", None),
            P(None, "shard", None),
        ),
        check_vma=False,
    )
```

```python
import functools
import math

import jax
import jax.numpy as jnp
from jax import lax
from jax.experimental import pallas as pl
from jax.experimental.pallas import tpu as pltpu
from jax.sharding import PartitionSpec as P

momentum_decay = 0.95
epsilon_norm = 1e-06
MESH = pl.DeviceIdType.MESH
HIGHEST = lax.Precision.HIGHEST
F32 = jnp.float32
BF16 = jnp.bfloat16
BLOCK = 64
PIVOTS = 4
CHUNKS = 8
TILES = 8


def grid_of(shards_n, replicas_n):
    x = math.isqrt(shards_n // 2)
    if x < 1 or 2 * x * x != shards_n:
        x = 1
    c = 2 if replicas_n % 2 == 0 else 1
    return shards_n // x, x, replicas_n // c, c


class Net:
    def __init__(self, dims, send, recv):
        self.dims = dims
        _, nx, _, nc = dims
        s = lax.axis_index("shard")
        r = lax.axis_index("replica")
        self.at = [s // nx, s % nx, r // nc, r % nc]
        self.send, self.recv, self.used = send, recv, 0

    def device(self, axis, coordinate):
        place = list(self.at)
        if axis is None:
            place[1], place[2] = coordinate
        else:
            place[axis] = coordinate
        return {
            "shard": place[0] * self.dims[1] + place[1],
            "replica": place[2] * self.dims[3] + place[3],
        }

    def peers(self, axis):
        n, me = self.dims[axis], self.at[axis]
        distances = sorted(range(1, n), key=lambda d: (min(d, n - d), d))
        return [((me + d) % n, (me + n - d) % n) for d in distances]

    def plane(self):
        nx, ny = self.dims[1:3]
        x, y = self.at[1:3]
        steps = sorted(((i, j) for i in range(nx) for j in range(ny) if i or j), key=lambda p: (min(p[0], nx - p[0]) + min(p[1], ny - p[1]), p))
        return [
            (((x + i) % nx, (y + j) % ny), ((x + nx - i) % nx, (y + ny - j) % ny)) for i, j in steps
        ]

    def barrier(self):
        sem = pltpu.get_barrier_semaphore()
        count = 0
        for axis in range(4):
            for target, _ in self.peers(axis):
                pl.semaphore_signal(sem, inc=1, device_id=self.device(axis, target), device_id_type=MESH)
                count += 1
        for target, _ in self.plane():
            pl.semaphore_signal(sem, inc=1, device_id=self.device(None, target), device_id_type=MESH)
            count += 1
        pl.semaphore_wait(sem, count)

    def start(self, src, dst, axis, target):
        i = self.used
        self.used += 1
        copy = pltpu.make_async_remote_copy(
            src_ref=src,
            dst_ref=dst,
            send_sem=self.send.at[i],
            recv_sem=self.recv.at[i],
            device_id=self.device(axis, target),
            device_id_type=MESH,
        )
        copy.start()
        return copy


def gather_all(net, own, out, work=None, use=None):
    z, x, y, c = net.at
    piece = out.shape[-2]
    a, b = pl.ds(0, piece // 2), pl.ds(piece // 2, piece - piece // 2)

    def pair(view, sent):
        for t, _ in net.peers(3):
            sent.append(net.start(view, view, 3, t))

    def spread(i, src):
        dst = out.at[i, x, y, c]
        along_x = [(net.start(src, dst, 1, t), f) for t, f in net.peers(1)]
        along_y = [(net.start(src, dst, 2, t), f) for t, f in net.peers(2)]
        sent = [net.start(src, dst, 3, t) for t, _ in net.peers(3)]
        return i, along_x, along_y, sent

    def relay(i, along_x, along_y, sent):
        corner = []
        for copy, f in along_x:
            copy.wait()
            view = out.at[i, f, y, c, a]
            corner += [(net.start(view, view, 2, t), out.at[i, f, g, c, a]) for t, g in net.peers(2)]
            pair(out.at[i, f, y, c], sent)
        for copy, f in along_y:
            copy.wait()
            view = out.at[i, x, f, c, b]
            corner += [(net.start(view, view, 1, t), out.at[i, g, f, c, b]) for t, g in net.peers(1)]
            pair(out.at[i, x, f, c], sent)
        return i, corner, sent

    along_z = [(net.start(own, out.at[z, x, y, c], 0, t), f) for t, f in net.peers(0)]
    first = spread(z, own)
    if work is not None:
        work()
    relayed = [relay(*first)]
    waves = []
    for copy, f in along_z:
        copy.wait()
        waves.append(spread(f, out.at[f, x, y, c]))
    relayed += [relay(*wave) for wave in waves]
    for i, corner, sent in relayed:
        for copy, view in corner:
            copy.wait()
            pair(view, sent)
    for i, corner, sent in relayed:
        for copy in sent:
            copy.wait()
        if use is not None:
            use(i)


def copies_of(dims):
    nz, nx, ny, nc = dims
    x, y, c = nx - 1, ny - 1, nc - 1
    gathered = (nz - 1) + nz * (x + y + c + x * (y + c) + y * (x + c) + 2 * x * y * c)
    summed = nz * (c + 2 * x * y + x + y + 1)
    return 2 * gathered + summed + 4 * c + 3 * y + 2 * nx * ny + nz + 8


def prefetch(momentum, grad, m, g, local):
    loads = []
    size = m.shape[0] // CHUNKS
    for k in range(CHUNKS):
        rows = pl.ds(k * size, size)
        pair = [
            pltpu.make_async_copy(momentum.at[rows], m.at[rows], local.at[2 * k + 1]),
            pltpu.make_async_copy(grad.at[rows], g.at[rows], local.at[2 * k + 2]),
        ]
        for copy in pair:
            copy.start()
        loads.append((rows, pair))
    return loads


def sum_left(net, part, left, gram, rc, acc, ry, g, rgc, g1, rg, g3, gz):
    z, x, y, c = net.at
    copies = [net.start(part.at[:, t], rc.at[d], 3, t) for d, (t, _) in enumerate(net.peers(3))]
    for copy in copies:
        copy.wait()
    total = part[:, c]
    for d in range(len(copies)):
        total = total + rc[d]
    acc[...] = total
    copies = [net.start(acc.at[t], ry.at[d], 2, t) for d, (t, _) in enumerate(net.peers(2))]
    for copy in copies:
        copy.wait()
    own = acc[y]
    for d in range(len(copies)):
        own = own + ry[d]
    left[y, c] = own
    rows = [net.start(left.at[y, c], left.at[y, c], 2, t) for t, _ in net.peers(2)]
    product = lax.dot_general(own, own, (((0,), (0,)), ((), ())), precision=HIGHEST, preferred_element_type=F32)
    g[...] = product.reshape(g.shape)
    copies = [net.start(g.at[t], rgc.at[d], 3, t) for d, (t, _) in enumerate(net.peers(3))]
    for copy in copies:
        copy.wait()
    total = g[c]
    for d in range(len(copies)):
        total = total + rgc[d]
    g1[...] = total
    copies = [net.start(g1.at[t[1], t[0]], rg.at[e], None, t) for e, (t, _) in enumerate(net.plane())]
    for copy in rows:
        copy.wait()
    rows = [net.start(left.at[:, c], left.at[:, c], 3, t) for t, _ in net.peers(3)]
    for copy in copies:
        copy.wait()
    total = g1[y, x]
    for e in range(len(copies)):
        total = total + rg[e]
    g3[...] = total
    gz[z] = total
    copies = [net.start(g3, gz.at[z], 0, t) for t, _ in net.peers(0)]
    for copy in copies:
        copy.wait()
    total = gz[0]
    for d in range(1, gz.shape[0]):
        total = total + gz[d]
    gram[c, y, x] = total
    view = gram.at[c, y, x]
    copies = [net.start(view, view, None, t) for t, _ in net.plane()]
    for copy in copies:
        copy.wait()
    copies = [net.start(gram.at[c], gram.at[c], 3, t) for t, _ in net.peers(3)]
    for copy in copies + rows:
        copy.wait()


def factor_inverse(block):
    n = block.shape[0]
    row = lax.broadcasted_iota(jnp.int32, (8, n), 0)
    lane = lax.broadcasted_iota(jnp.int32, (8, n), 1)
    parts = [
        jnp.concatenate([block[8 * i : 8 * i + 8, :], jnp.where(lane == row + 8 * i, 1.0, 0.0).astype(F32)], axis=1)
        for i in range(n // 8)
    ]
    ids = lax.broadcasted_iota(jnp.int32, (8, 2 * n), 0)
    for j in range(0, n, PIVOTS):
        first, o = j // 8, j % 8
        head = parts[first]
        s = {}
        for p in range(PIVOTS):
            for q in range(p, PIVOTS):
                s[p, q] = jnp.broadcast_to(head[o + p : o + p + 1, j + q : j + q + 1], (1, 2 * n))
        rows = [head[o + p : o + p + 1, :] for p in range(PIVOTS)]
        cols = [
            [jnp.broadcast_to(part[:, j + p : j + p + 1], (8, 2 * n)) for part in parts[first:]]
            for p in range(PIVOTS)
        ]
        total = None
        done = []
        for p in range(PIVOTS):
            r = lax.rsqrt(s[p, p])
            inv = r * r
            for q in range(p + 1, PIVOTS):
                t = s[p, q] * inv
                rows[q] = rows[q] - t * rows[p]
                cols[q] = [cq - t * cp for cq, cp in zip(cols[q], cols[p])]
                for w in range(q, PIVOTS):
                    s[q, w] = s[q, w] - t * s[p, w]
            done.append(rows[p] * r)
            scaled = rows[p] * inv
            terms = [cp * scaled for cp in cols[p]]
            total = terms if total is None else [u + v for u, v in zip(total, terms)]
        head = jnp.where(ids >= o + PIVOTS, head - total[0], head)
        for p in range(PIVOTS):
            head = jnp.where(ids == o + p, done[p], head)
        rest = [part - u for part, u in zip(parts[first + 1 :], total[1:])]
        parts = parts[:first] + [head] + rest
    return jnp.concatenate(parts, axis=0)[:, n:]


def orthonormal(gram, left, ortho, rounded, work, inverse):
    n = gram.shape[-1]
    row = lax.broadcasted_iota(jnp.int32, (n, n), 0)
    col = lax.broadcasted_iota(jnp.int32, (n, n), 1)
    work[:, :n] = gram[...].reshape(n, n)
    work[:, n:] = jnp.where(row == col, 1.0, 0.0).astype(F32)
    inverse[...] = jnp.zeros((n, n), F32)
    for lo in range(0, n, BLOCK):
        hi = lo + BLOCK
        start, end = hi // 128 * 128, (n + hi + 127) // 128 * 128
        corner = factor_inverse(work[lo:hi, lo:hi])
        upper = jnp.dot(corner, work[lo:hi, start:end], precision=HIGHEST, preferred_element_type=F32)
        inverse[lo:hi, : end - n] = upper[:, n - start :]
        if hi < n:
            work[hi:, start:end] -= lax.dot_general(
                upper[:, hi - start : n - start], upper, (((0,), (0,)), ((), ())),
                precision=HIGHEST, preferred_element_type=F32,
            )
    result = lax.dot_general(
        left[...].reshape(ortho.shape), inverse[...], (((1,), (1,)), ((), ())), precision=HIGHEST, preferred_element_type=F32
    )
    ortho[...] = result
    rounded[...] = result.astype(BF16)


def sum_right(net, use, buffer, ortho, out, part, sc, rc, acc, sa, ra, sb, rb, sx, rx, sy, ry, sz, rz, own):
    nz, nx, ny, nc = net.dims
    z, x, y, c = net.at
    xs, ys, cs = net.peers(1), net.peers(2), net.peers(3)
    targets = [t for t, _ in reversed(net.peers(0))] + [z]
    half = acc.shape[-2] // 2
    wide = buffer.shape[1] // nz
    corners = [(i, j) for j in range(ny - 1) for i in range(nx - 1)]
    pending = {}

    def multiply(k):
        columns = pl.ds(pl.multiple_of(targets[k] * wide, 128), wide)
        product = lax.dot_general(
            buffer[:, columns], ortho[...], (((0,), (0,)), ((), ())), preferred_element_type=F32
        )
        part[k] = product.reshape(part.shape[1:])
        copies = []
        for d, (t, _) in enumerate(cs):
            sc[d, k] = part[k, :, :, t].astype(BF16)
            copies.append(net.start(sc.at[d, k], rc.at[d, k], 3, t))
        pending[k] = copies

    def corner(k):
        for copy in pending[k]:
            copy.wait()
        total = part[k, :, :, c]
        for d in range(nc - 1):
            total = total + rc[d, k].astype(F32)
        acc[k] = total
        copies = []
        for e, (i, j) in enumerate(corners):
            tx, ty = xs[i][0], ys[j][0]
            sa[e, k] = acc[k, tx, ty, :half].astype(BF16)
            copies.append(net.start(sa.at[e, k], ra.at[e, k], 2, ty))
            sb[e, k] = acc[k, tx, ty, half:].astype(BF16)
            copies.append(net.start(sb.at[e, k], rb.at[e, k], 1, tx))
        pending[k] = copies

    def across(k):
        for copy in pending[k]:
            copy.wait()
        copies = []
        for i, (tx, _) in enumerate(xs):
            low = acc[k, tx, y, :half]
            for e, (p, _) in enumerate(corners):
                if p == i:
                    low = low + ra[e, k].astype(F32)
            sx[i, k, :half] = low.astype(BF16)
            sx[i, k, half:] = acc[k, tx, y, half:].astype(BF16)
            copies.append(net.start(sx.at[i, k], rx.at[i, k], 1, tx))
        for j, (ty, _) in enumerate(ys):
            high = acc[k, x, ty, half:]
            for e, (_, q) in enumerate(corners):
                if q == j:
                    high = high + rb[e, k].astype(F32)
            sy[j, k, :half] = acc[k, x, ty, :half].astype(BF16)
            sy[j, k, half:] = high.astype(BF16)
            copies.append(net.start(sy.at[j, k], ry.at[j, k], 2, ty))
        pending[k] = copies

    def along(k):
        for copy in pending[k]:
            copy.wait()
        total = acc[k, x, y]
        for i in range(nx - 1):
            total = total + rx[i, k].astype(F32)
        for j in range(ny - 1):
            total = total + ry[j, k].astype(F32)
        if k == nz - 1:
            return total
        sz[k] = total.astype(BF16)
        pending[k] = [net.start(sz.at[k], rz.at[k], 0, targets[k])]
        return None

    total = None
    for step in range(nz + 3):
        for lag, phase in ((3, along), (2, across), (1, corner), (0, multiply)):
            if 0 <= step - lag < nz:
                total = phase(step - lag)
                if lag == 3:
                    final = total
    for k in range(nz - 1):
        for copy in pending[k]:
            copy.wait()
        final = final + rz[k].astype(F32)
    mine = (final * (1.0 / (ny * nc))).astype(BF16)
    own[...] = mine
    out[z, x, y, c] = mine
    gather_all(net, own, out, use=use)


def kernel(dims, block, momentum, grad, right, ortho, rounded, moved, squares, prev, buffer, m, g, part, left, gram, *rest):
    lefts, (work, inverse), rights = rest[:9], rest[9:11], rest[11:-3]
    send, recv, local = rest[-3:]
    net = Net(dims, send, recv)
    z, x, y, c = net.at
    own = pltpu.make_async_copy(block.at[y, c], prev.at[z, x, y, c], local.at[0])
    own.start()
    loads = prefetch(momentum, grad, m, g, local)
    net.barrier()
    own.wait()

    def add():
        for rows, pair in loads:
            for copy in pair:
                copy.wait()
            buffer[rows, :] = (m[rows, :].astype(F32) + g[rows, :].astype(F32)).astype(BF16)

    gather_all(net, block.at[y, c], prev, add)
    width = buffer.shape[1]
    product = jnp.dot(buffer[...], prev[...].reshape(width, prev.shape[-1]), preferred_element_type=F32)
    part[...] = product.reshape(part.shape)
    sum_left(net, part, left, gram, *lefts)
    orthonormal(gram, left, ortho, rounded, work, inverse)
    squares[...] = jnp.zeros(squares.shape, F32)
    wide = width // dims[0]
    size = min(wide, 512)

    def use(i):
        rows = right[i].reshape(wide, right.shape[-1])
        square = rows.astype(F32)
        squares[0:1] = squares[0:1] + jnp.sum(square * square, axis=0, keepdims=True)
        for k in range(0, wide, size):
            columns = pl.ds(pl.multiple_of(i * wide + k, 128), size)
            feedback = lax.dot_general(
                rounded[...], rows[k : k + size], (((1,), (1,)), ((), ())), preferred_element_type=F32
            )
            total = m[:, columns].astype(F32) + g[:, columns].astype(F32)
            moved[:, columns] = (total - (1.0 - momentum_decay) * feedback).astype(BF16)

    sum_right(net, use, buffer, rounded, right, *rights)


def finish_kernel(factor, right, ortho, moved, squares, momentum_new, update, own, stage, sem):
    rows, rank = ortho.shape
    width = right.shape[0]
    first = pltpu.make_async_copy(moved, momentum_new, sem.at[0])
    first.start()
    start = pl.multiple_of(lax.axis_index("shard") * rows, rows)
    second = pltpu.make_async_copy(right.at[pl.ds(start, rows)], own, sem.at[1])
    second.start()
    norms = jnp.sqrt(squares[0:1, :] + epsilon_norm)
    scaled = (ortho[...] * (factor / norms)).astype(BF16)
    size = width // TILES
    copies = [first, second]
    for k in range(TILES):
        columns = slice(k * size, (k + 1) * size)
        stage[k] = lax.dot_general(
            scaled, right[columns, :], (((1,), (1,)), ((), ())), preferred_element_type=F32
        ).astype(BF16)
        copy = pltpu.make_async_copy(stage.at[k], update.at[:, columns], sem.at[2 + k])
        copy.start()
        copies.append(copy)
    for copy in copies:
        copy.wait()


def finish(right, ortho, moved, squares):
    width, rank = right.shape
    rows = ortho.shape[0]
    vmem = pl.BlockSpec(memory_space=pltpu.VMEM)
    hbm = pl.BlockSpec(memory_space=pltpu.MemorySpace.HBM)
    return pl.pallas_call(
        functools.partial(finish_kernel, width / math.sqrt(rank)),
        out_shape=(
            jax.ShapeDtypeStruct(moved.shape, BF16),
            jax.ShapeDtypeStruct(moved.shape, BF16),
            jax.ShapeDtypeStruct((rows, rank), BF16),
        ),
        in_specs=[vmem] * 4,
        out_specs=(hbm, hbm, hbm),
        scratch_shapes=[
            pltpu.VMEM((TILES, rows, width // TILES), BF16),
            pltpu.SemaphoreType.DMA((2 + TILES,)),
        ],
        compiler_params=pltpu.CompilerParams(vmem_limit_bytes=12 << 20),
    )(right, ortho, moved, squares)


def factors(dims, block, momentum, grad):
    nz, nx, ny, nc = dims
    rows, rank = block.shape
    width = momentum.shape[1]
    lp = rows // (ny * nc)
    rp = width // (nz * nx * ny * nc)
    gr = rank // (nc * ny * nx)
    pc, py, px, pz = max(nc - 1, 1), max(ny - 1, 1), max(nx - 1, 1), max(nz - 1, 1)
    pe, half = px * py, rp // 2
    full = (nz, nx, ny, nc, rp, rank)
    scratch = [
        ((nz, nx, ny, nc, lp, rank), BF16), (momentum.shape, BF16), (momentum.shape, BF16), (momentum.shape, BF16),
        ((ny, nc, lp, rank), F32), ((ny, nc, lp, rank), F32), ((nc, ny, nx, gr, rank), F32),
        ((pc, ny, lp, rank), F32), ((ny, lp, rank), F32), ((py, lp, rank), F32),
        ((nc, ny, nx, gr, rank), F32), ((pc, ny, nx, gr, rank), F32), ((ny, nx, gr, rank), F32),
        ((max(nx * ny - 1, 1), gr, rank), F32), ((gr, rank), F32),
        ((nz, gr, rank), F32),
        ((rank, 2 * rank), F32), ((rank, rank), F32),
        (full, F32),
        ((pc, nz, nx, ny, rp, rank), BF16), ((pc, nz, nx, ny, rp, rank), BF16),
        ((nz, nx, ny, rp, rank), F32),
        ((pe, nz, half, rank), BF16), ((pe, nz, half, rank), BF16),
        ((pe, nz, rp - half, rank), BF16), ((pe, nz, rp - half, rank), BF16),
        ((px, nz, rp, rank), BF16), ((px, nz, rp, rank), BF16),
        ((py, nz, rp, rank), BF16), ((py, nz, rp, rank), BF16),
        ((pz, rp, rank), BF16), ((pz, rp, rank), BF16),
        ((rp, rank), BF16),
    ]
    copies = copies_of(dims)
    vmem = pl.BlockSpec(memory_space=pltpu.VMEM)
    hbm = pl.BlockSpec(memory_space=pltpu.MemorySpace.HBM)
    right, ortho, _, moved, squares = pl.pallas_call(
        functools.partial(kernel, dims),
        out_shape=(
            jax.ShapeDtypeStruct(full, BF16),
            jax.ShapeDtypeStruct((rows, rank), F32),
            jax.ShapeDtypeStruct((rows, rank), BF16),
            jax.ShapeDtypeStruct(momentum.shape, BF16),
            jax.ShapeDtypeStruct((8, rank), F32),
        ),
        in_specs=[vmem, hbm, hbm],
        out_specs=(vmem,) * 5,
        scratch_shapes=[pltpu.VMEM(shape, kind) for shape, kind in scratch]
        + [pltpu.SemaphoreType.DMA((copies,))] * 2
        + [pltpu.SemaphoreType.DMA((2 * CHUNKS + 1,))],
        compiler_params=pltpu.CompilerParams(
            collective_id=0, has_side_effects=True, vmem_limit_bytes=36 << 20
        ),
    )(block.reshape(ny, nc, lp, rank), pltpu.with_memory_space_constraint(momentum, pltpu.MemorySpace.HBM), pltpu.with_memory_space_constraint(grad, pltpu.MemorySpace.HBM))
    return right.reshape(width, rank), ortho, moved, squares


def shards(dims, momentum, grad, right_prev):
    right, ortho, moved, squares = factors(dims, right_prev[0], momentum[0, 0], grad[0, 0])
    momentum_new, update, right_own = finish(right, ortho, moved, squares)
    return momentum_new[None, None], update[None], right_own[None]


def solution(mesh):
    dims = grid_of(mesh.shape["shard"], mesh.shape["replica"])
    return jax.shard_map(
        functools.partial(shards, dims),
        mesh=mesh,
        in_specs=(
            P(None, "replica", "shard", None),
            P(None, "replica", "shard", None),
            P(None, "shard", None),
        ),
        out_specs=(
            P(None, "replica", "shard", None),
            P(None, "shard", None),
            P(None, "shard", None),
        ),
        check_vma=False,
    )
```
